128 devices in a mesh: hst: 4 (over y), chip: 32 (over x, z, core).
Axes of the slice: x: 4, y: 4, z: 4, core: 2. Of those that a mesh axis runs over, the one named last changes fastest.
Arguments:
- resident_row_blocks: bfloat16 [6144, 128, 128], P(('hst', 'chip')), may hold values from -3 to 3
- orphan_blocks: bfloat16 [4096, 128, 128], P(('hst', 'chip')), may hold values from -3 to 3
- home_offsets: int32 [6144, 128, 8], P(('hst', 'chip')), may hold values from 0 to 127
- home_lengths: int32 [6144, 128], P(('hst', 'chip')), may hold values from 1 to 8
- home_samples: int32 [6144, 128], P(('hst', 'chip')), may hold values from 0 to 511
- orphan_offsets: int32 [4096, 128, 8], P(('hst', 'chip')), may hold values from 0 to 127
- orphan_lengths: int32 [4096, 128], P(('hst', 'chip')), may hold values from 1 to 8
- orphan_samples: int32 [4096, 128], P(('hst', 'chip')), may hold values from 0 to 511
- orphan_owner: int32 [4096, 1], P(('hst', 'chip')), may hold values from 0 to 31; in each aligned block of 32 rows (0 to 31, 32 to 63, ...) at most 2 rows name the same one
- dense_inputs: bfloat16 [65536, 13], P(('hst', 'chip')), may hold values from -6 to 6
- labels: int32 [65536], P(('hst', 'chip')), may hold values 0 or 1
- bottom_first: bfloat16 [13, 512], replicated, may hold values from -1.75 to 1.75
- bias_first: float32 [512], replicated, may hold values from -1.5 to 1.5
- bottom_second: bfloat16 [512, 256], replicated, may hold values from -0.375 to 0.375
- bias_second: float32 [256], replicated, may hold values from -1.5 to 1.5
- bottom_third: bfloat16 [256, 128], replicated, may hold values from -0.5 to 0.5
- bias_third: float32 [128], replicated, may hold values from -1.5 to 1.5
- top_hidden: bfloat16 [479, 1024], replicated, may hold values from -0.125 to 0.125
- bias_hidden: float32 [1024], replicated, may hold values from -1.5 to 1.5
- top_logit: bfloat16 [1024, 1], replicated, may hold values from -0.25 to 0.25
- bias_logit: float32 [1], replicated, may hold values from -3 to 3
Outputs:
- rehomed: bfloat16 [8192, 128, 128], P(('hst', 'chip'))
- logits: float32 [65536], P(('hst', 'chip'))
- loss: float32 [], replicated
The draws below stay inside these ranges and needn't reach their ends.
Inputs may be any that keep to these rules, and one draw needn't show every extreme that they name: `orphan_owner`: among the 32 orphans of one device at most 2 have the same new owner; some holder and owner reach 2.
All inputs are finite; a program needn't handle non-finite values. No bound on the sum of `labels` on one device may be relied on, other than what follows from the above.
Results may differ from the reference program's by a relative error of at most 0.0079.
Values may be sent and summed in bfloat16 or wider, within the bound.
No kernel may reach another device: no remote copies, remote signals or barrier semaphores. Data moves between devices by JAX's collectives and lax.ppermute only.
A program may use at most 128 MiB of HBM per device.

```python
import math
import jax
import jax.numpy as jnp
import numpy as np
from jax import lax

E = 128
F = 26
DENSE = 13
BOT1 = 512
BOT2 = 256
TOP1 = 1024
BR = 128
L = 8
ORPH_DEV = 32
BATCH_DEV = 512
SLOT = 2
RECV = 64
PIECES = 128
RESIDENT = 6144
ORPHANS = 4096
BATCH = 65536
INTER = 479
N_HST = 4
N_CHIP = 32
DEVICES = 128


def touch_ends(result, stream_key, low, high):
    shape = result.shape
    index_at = [jax.random.randint(jax.random.fold_in(stream_key, axis), (), 0, shape[axis]) for axis in range(len(shape))]
    result = result.at[tuple(index_at)].set(low)
    longest = shape.index(max(shape))
    index_at[longest] = (index_at[longest] + 1) % shape[longest]
    return result.at[tuple(index_at)].set(high)


def levels(rng, dims, cuts, low, top_value):
    loudness = 1.0
    for position, blocks in cuts:
        steps = jax.random.uniform(jax.random.fold_in(jax.random.fold_in(rng, 6), position), (blocks,), jnp.float32, low / len(cuts), top_value / len(cuts))
        loudness = loudness * jnp.repeat(jnp.exp(steps), dims[position] // blocks).reshape((-1,) + (1,) * (len(dims) - 1 - position))
    return loudness


def shared_out(own_key, own, number, rows, number_of, top, bound, slope):
    ranking = jax.random.permutation(own_key, number_of)
    heavy_load, ordinary = portions_of(number_of, rows * top, bound, slope, True), portions_of(number_of, rows * top, bound, slope, False)
    places = jnp.arange(number_of)

    def named(tallies, turn):
        used = int((tallies > 0).sum())
        fixed = max(1, used // 4)
        shifted = fixed + (places - fixed + turn * (used - fixed)) % max(1, number_of - fixed)
        return jnp.zeros((number_of,), jnp.int32).at[ranking[jnp.where(places < fixed, places, shifted)]].set(jnp.asarray(tallies, jnp.int32))

    tallies = jnp.where(number % 4 == 0, named(heavy_load, number // 4), named(ordinary, number - number // 4 - 1))
    mixed = jax.random.permutation(jax.random.fold_in(own, 3), number_of)
    donor, taker = mixed[0:number_of // 2 * 2:2], mixed[1:number_of // 2 * 2:2]
    slack = jnp.minimum(tallies[donor] - 1, bound - tallies[taker]) // 2
    slack = jnp.where((donor == ranking[0]) | (taker == ranking[0]) | (tallies[taker] == 0), 0, jnp.maximum(slack, 0))
    shifted = jax.random.randint(jax.random.fold_in(own, 4), (number_of // 2,), 0, 1 << 20) % (slack + 1)
    tallies = tallies.at[donor].add(-shifted).at[taker].add(shifted)
    items = jnp.searchsorted(jnp.cumsum(tallies), jnp.arange(rows * top), side="right").astype(jnp.int32)
    listing = items.reshape(top, rows).T
    listing = listing[jax.random.permutation(jax.random.fold_in(own, 1), rows)]
    turn = jax.random.randint(jax.random.fold_in(own, 2), (rows, 1), 0, top)
    return jnp.take_along_axis(listing, (jnp.arange(top)[None, :] + turn) % top, axis=1)


def portions_of(count, total, limit, slope, full):
    portions = [(1 << 20) // math.isqrt(standing ** slope) + 1 for standing in range(1, count + 1)]
    largest = limit if full else min(limit, max(-(-total // count), total * portions[0] // sum(portions)))
    least = 1 if total - largest >= count - 1 else 0
    given, surplus = [largest] + [least] * (count - 1), total - largest - least * (count - 1)
    while surplus > 0:
        candidates = [i for i in range(1, count) if given[i] < largest] or [i for i in range(1, count) if given[i] < limit]
        mass, remaining = sum([portions[i] for i in candidates]), surplus
        for i in candidates:
            addition = min(limit - given[i], max(1, remaining * portions[i] // mass), surplus)
            given[i] = given[i] + addition
            surplus = surplus - addition
    return np.array(given)


def gaussian(key, dims, scale, reach, split=(), held_as=jnp.bfloat16):
    values = jax.random.normal(key, dims, jnp.float32) * scale
    if len(split) > 0:
        values = levels(key, dims, split, -0.22, 0.18) * values
    return jnp.clip(values, min=-reach, max=reach).astype(held_as)


def setup_inputs(seed: int = 0) -> dict:
    seeds = jax.random.split(jax.random.key(seed), 22)
    resident_row_blocks = gaussian(seeds[0], (RESIDENT, BR, E), 0.5, 3.0, ((0, 128),))
    orphan_blocks = gaussian(seeds[1], (ORPHANS, BR, E), 0.5, 3.0, ((0, 128),))
    home_offsets = touch_ends(jax.random.randint(seeds[2], (RESIDENT, PIECES, L), 0, BR), jax.random.fold_in(seeds[2], 1), 0, BR - 1).astype(jnp.int32)
    home_lengths = touch_ends(jax.random.randint(seeds[3], (RESIDENT, PIECES), 1, L + 1), jax.random.fold_in(seeds[3], 1), 1, L).astype(jnp.int32)
    home_samples = touch_ends(jax.random.randint(seeds[4], (RESIDENT, PIECES), 0, BATCH_DEV), jax.random.fold_in(seeds[4], 1), 0, BATCH_DEV - 1).astype(jnp.int32)
    orphan_offsets = touch_ends(jax.random.randint(seeds[5], (ORPHANS, PIECES, L), 0, BR), jax.random.fold_in(seeds[5], 1), 0, BR - 1).astype(jnp.int32)
    orphan_lengths = touch_ends(jax.random.randint(seeds[6], (ORPHANS, PIECES), 1, L + 1), jax.random.fold_in(seeds[6], 1), 1, L).astype(jnp.int32)
    orphan_samples = touch_ends(jax.random.randint(seeds[7], (ORPHANS, PIECES), 0, BATCH_DEV), jax.random.fold_in(seeds[7], 1), 0, BATCH_DEV - 1).astype(jnp.int32)
    orphan_owner_keys = jax.random.split(jax.random.fold_in(seeds[8], 1), ORPHANS // ORPH_DEV)
    orphan_owner_turns = jax.random.permutation(jax.random.fold_in(seeds[8], 3), ORPHANS // ORPH_DEV)
    orphan_owner = jax.vmap(lambda own, number: shared_out(jax.random.fold_in(seeds[8], 2), own, number, ORPH_DEV, N_CHIP, 1, SLOT, 2))(orphan_owner_keys, orphan_owner_turns).reshape((ORPHANS, 1))
    dense_inputs = gaussian(seeds[9], (BATCH, DENSE), 1.0, 6.0, ((0, 128),))
    labels = touch_ends((jax.random.randint(seeds[10], (BATCH,), 0, 2) < 1).astype(jnp.int32), jax.random.fold_in(seeds[10], 1), 0, 1)
    bottom_first = gaussian(seeds[11], (DENSE, BOT1), DENSE ** -0.5, 1.75)
    bias_first = gaussian(seeds[12], (BOT1,), 0.3, 1.5, (), jnp.float32)
    bottom_second = gaussian(seeds[13], (BOT1, BOT2), (BOT1 // 2) ** -0.5, 0.375)
    bias_second = gaussian(seeds[14], (BOT2,), 0.3, 1.5, (), jnp.float32)
    bottom_third = gaussian(seeds[15], (BOT2, E), (BOT2 // 2) ** -0.5, 0.5)
    bias_third = gaussian(seeds[16], (E,), 0.3, 1.5, (), jnp.float32)
    top_hidden = gaussian(seeds[17], (INTER, TOP1), (INTER * 4) ** -0.5, 0.125)
    bias_hidden = gaussian(seeds[18], (TOP1,), 0.3, 1.5, (), jnp.float32)
    top_logit = gaussian(seeds[19], (TOP1, 1), (TOP1 // 2) ** -0.5, 0.25)
    bias_logit = gaussian(seeds[20], (1,), 1.0, 3.0, (), jnp.float32)
    return dict(resident_row_blocks=resident_row_blocks, orphan_blocks=orphan_blocks, home_offsets=home_offsets, home_lengths=home_lengths, home_samples=home_samples, orphan_offsets=orphan_offsets, orphan_lengths=orphan_lengths, orphan_samples=orphan_samples, orphan_owner=orphan_owner, dense_inputs=dense_inputs, labels=labels, bottom_first=bottom_first, bias_first=bias_first, bottom_second=bottom_second, bias_second=bias_second, bottom_third=bottom_third, bias_third=bias_third, top_hidden=top_hidden, bias_hidden=bias_hidden, top_logit=top_logit, bias_logit=bias_logit)


def pool_one(block, offsets, lengths):
    rows = jnp.arange(block.shape[0], dtype=jnp.int32)
    places = jnp.arange(offsets.shape[1], dtype=jnp.int32)
    hit = (offsets[:, :, None] == rows[None, None, :]) & (places[None, :, None] < lengths[:, None, None])
    counts = jnp.sum(hit.astype(jnp.float32), axis=1)
    return jnp.dot(counts.astype(jnp.bfloat16), block, preferred_element_type=jnp.float32).astype(jnp.bfloat16)


def slot_provenance(owners):
    count = owners.shape[0]
    index = jnp.arange(count, dtype=jnp.int32)
    earlier = index[None, :] < index[:, None]
    rank = jnp.sum(((owners[:, None] == owners[None, :]) & earlier).astype(jnp.int32), axis=1).astype(jnp.int32)
    flat = owners * SLOT + rank
    match = flat[None, :] == jnp.arange(RECV, dtype=jnp.int32)[:, None]
    source = jnp.sum(match.astype(jnp.int32) * index[None, :], axis=1).astype(jnp.int32)
    return source, jnp.any(match, axis=1)


def reference(resident_row_blocks, orphan_blocks, home_offsets, home_lengths, home_samples, orphan_offsets, orphan_lengths, orphan_samples, orphan_owner, dense_inputs, labels, bottom_first, bias_first, bottom_second, bias_second, bottom_third, bias_third, top_hidden, bias_hidden, top_logit, bias_logit):
    grouped = orphan_blocks.reshape(DEVICES, ORPH_DEV, BR, E)
    owners = orphan_owner[:, 0].reshape(DEVICES, ORPH_DEV)

    def outgoing(blocks, targets):
        source, filled = slot_provenance(targets)
        return jnp.where(filled[:, None, None], blocks[source], jnp.zeros((), jnp.bfloat16))

    buffers = jax.vmap(outgoing)(grouped, owners)
    buffers = buffers.reshape(N_HST, N_CHIP, N_CHIP, SLOT, BR, E).transpose(0, 2, 1, 3, 4, 5)
    rehomed = buffers.reshape(DEVICES * RECV, BR, E)

    blocks = jnp.concatenate([resident_row_blocks, orphan_blocks], axis=0)
    offsets = jnp.concatenate([home_offsets, orphan_offsets], axis=0)
    lengths = jnp.concatenate([home_lengths, orphan_lengths], axis=0)
    samples = jnp.concatenate([home_samples, orphan_samples], axis=0)
    ids = jnp.arange(blocks.shape[0], dtype=jnp.int32)
    feature = ids % F
    piece = lax.map(lambda item: pool_one(item[0], item[1], item[2]), (blocks, offsets, lengths))
    owner = jnp.arange(PIECES, dtype=jnp.int32)
    target = (owner[None, :] * BATCH_DEV + samples) * F + feature[:, None]
    pooled = jax.ops.segment_sum(piece.reshape(-1, E).astype(jnp.float32), target.reshape(-1).astype(jnp.int32), num_segments=BATCH * F)
    pooled = pooled.reshape(BATCH, F, E)

    first = jax.nn.relu(jnp.dot(dense_inputs, bottom_first, preferred_element_type=jnp.float32) + bias_first).astype(jnp.bfloat16)
    second = jax.nn.relu(jnp.dot(first, bottom_second, preferred_element_type=jnp.float32) + bias_second).astype(jnp.bfloat16)
    bottom = jax.nn.relu(jnp.dot(second, bottom_third, preferred_element_type=jnp.float32) + bias_third)
    stacked_vectors = jnp.concatenate([bottom[:, None, :], pooled], axis=1).astype(jnp.bfloat16)
    widened_features = stacked_vectors.astype(jnp.float32)
    pairwise_products = jnp.einsum("asu,adu->asd", widened_features, widened_features)
    lower_i, lower_j = np.tril_indices(F + 1, -1)
    pairs = pairwise_products[:, lower_i, lower_j]
    feature_vectors = jnp.concatenate([bottom, pairs], axis=1).astype(jnp.bfloat16)
    hidden = jax.nn.relu(jnp.dot(feature_vectors, top_hidden, preferred_element_type=jnp.float32) + bias_hidden).astype(jnp.bfloat16)
    logits = jnp.dot(hidden, top_logit, preferred_element_type=jnp.float32)[:, 0] + bias_logit[0]
    loss = jnp.sum(jax.nn.softplus(logits) - labels.astype(jnp.float32) * logits)
    return rehomed, logits, loss
```

```python
import functools

import jax
import jax.numpy as jnp
import numpy as np
from jax import lax
from jax.experimental import pallas as pl
from jax.experimental.pallas import tpu as pltpu
from jax.sharding import PartitionSpec as P

ALL = ("hst", "chip")
PERIOD = 13
HOME, ORPHAN = 48, 32
FIXED = 6
SLOTS = 84
ROWS = 88
F = 26
BATCH = 512
NONE = 1023
QW = 896
BF, F32 = jnp.bfloat16, jnp.float32
VMEM = pl.BlockSpec(memory_space=pltpu.VMEM)
SMEM = pl.BlockSpec(memory_space=pltpu.SMEM)


def slot_tables():
    table = np.full((PERIOD, 128), -1, np.int32)
    label = np.full((PERIOD, 3), -1, np.int32)
    for r in range(PERIOD):
        for g in range(PERIOD):
            k = (g - 11 * r) % PERIOD
            o = (g - 4 - 3 * r) % PERIOD
            for e in range(2):
                table[r, FIXED * g + e] = 2 * k + e
                if k + PERIOD < HOME // 2:
                    table[r, FIXED * g + 2 + e] = 2 * (k + PERIOD) + e
                table[r, FIXED * g + 4 + e] = 2 * o + e
        rest = [(PERIOD + i, (4 + 3 * r + i) % PERIOD) for i in range(3)]
        free = [0, 1, 2]
        for k, g in sorted(rest, key=lambda item: item[1] == 0):
            at = g % 3 if g % 3 in free else free[0]
            free.remove(at)
            label[r, at] = g
            for e in range(2):
                table[r, PERIOD * FIXED + 2 * at + e] = 2 * k + e
    for g in range(1, PERIOD):
        assert all(at == g % 3 for r in range(PERIOD) for at in range(3) if label[r, at] == g)
    return table, label


def feature_rows():
    rows = np.full((QW,), 479, np.int32)
    rows[:128] = np.arange(128)
    at = 128
    for a in range(4):
        for tile in range(1 if a < 2 else 2):
            for lane in range(128):
                turn = (lane - 7) % 128
                i, j = 8 * a + turn % 8, 16 * tile + turn // 8
                if j < i <= F:
                    rows[at + lane] = 128 + i * (i - 1) // 2 + j
            at += 128
    return rows


TABLE, LABEL = slot_tables()
FEATURE_ROWS = feature_rows()


def route_kernel(owner, orphans, out, count):
    slots = out.shape[0] // count.shape[0]

    def clear(c, _):
        count[c] = 0
        return 0

    lax.fori_loop(0, count.shape[0], clear, 0)
    out[...] = jnp.zeros_like(out)

    def place(i, _):
        o = owner[i]
        n = count[o]
        out[slots * o + n] = orphans[i]
        count[o] = n + 1
        return 0

    lax.fori_loop(0, orphans.shape[0], place, 0)


def route(orphan_owner, orphans, chips):
    return pl.pallas_call(
        route_kernel,
        out_shape=jax.ShapeDtypeStruct((2 * chips,) + orphans.shape[1:], BF),
        in_specs=[SMEM, VMEM],
        out_specs=VMEM,
        scratch_shapes=[pltpu.SMEM((chips,), jnp.int32)],
        compiler_params=pltpu.CompilerParams(vmem_limit_bytes=16 << 20),
        cost_estimate=pl.CostEstimate(flops=0, transcendentals=0, bytes_accessed=3 << 20),
    )(orphan_owner, orphans)


def pool_kernel(tab, home, orphan, home_off, home_len, home_sam, orphan_off, orphan_len, orphan_sam, out, wide, sam):
    rows = lax.broadcasted_iota(jnp.int32, (128, 128), 0).astype(F32).astype(BF)
    place = lax.broadcasted_iota(jnp.int32, (8, 128), 0)
    one, zero = jnp.ones((), BF), jnp.zeros((), BF)
    sam[...] = jnp.zeros_like(sam)

    def piece(slot, blocks, off, length, samples):
        at = tab[slot]
        b = jnp.maximum(at, 0)
        live = jnp.where(place < length[pl.ds(b, 1), :], off[b], -1).astype(F32).astype(BF)
        counts = jnp.zeros((128, 128), BF)
        for n in range(8):
            counts = counts + jnp.where(rows == live[n : n + 1, :], one, zero)
        sums = lax.dot_general(counts, blocks[b], (((0,), (0,)), ((), ())), preferred_element_type=F32)
        wide[pl.ds(slot, 128, stride=ROWS), :] = sums
        sam[pl.ds(slot, 1), :] = jnp.where(at >= 0, samples[pl.ds(b, 1), :], NONE)

    def group(g, _):
        for e in range(4):
            piece(FIXED * g + e, home, home_off, home_len, home_sam)
        for e in range(4, 6):
            piece(FIXED * g + e, orphan, orphan_off, orphan_len, orphan_sam)
        return 0

    lax.fori_loop(0, PERIOD, group, 0)

    def last(s, _):
        piece(PERIOD * FIXED + s, orphan, orphan_off, orphan_len, orphan_sam)
        return 0

    lax.fori_loop(0, 6, last, 0)
    index = sam[...]
    wide[pl.ds(SLOTS, 128, stride=ROWS), :] = (index >> 4).astype(F32).T
    wide[pl.ds(SLOTS + 1, 128, stride=ROWS), :] = (index & 15).astype(F32).T
    for s in range(SLOTS + 2, ROWS):
        wide[pl.ds(s, 128, stride=ROWS), :] = jnp.zeros((128, 128), F32)

    def narrow(q, _):
        out[pl.ds(4 * q, 4)] = wide[pl.ds(4 * q * ROWS, 4 * ROWS), :].reshape(4, ROWS, 128).astype(BF)
        return 0

    lax.fori_loop(0, 32, narrow, 0)


def pool(tab, *arrays):
    return pl.pallas_call(
        pool_kernel,
        out_shape=jax.ShapeDtypeStruct((128, ROWS, 128), BF),
        in_specs=[SMEM] + [VMEM] * 8,
        out_specs=VMEM,
        scratch_shapes=[pltpu.VMEM((128 * ROWS, 128), F32), pltpu.VMEM((128, 128), jnp.int32)],
        compiler_params=pltpu.CompilerParams(vmem_limit_bytes=24 << 20),
        cost_estimate=pl.CostEstimate(flops=84 * 128 * 128 * 256, transcendentals=0, bytes_accessed=6 << 20),
    )(tab, *arrays)


def tail_kernel(label, recv, bottom, weights, bias, last, last_bias, marks, logits, loss, wide, hi, lo, stack, turned, packed):
    zero = jnp.zeros((), BF)
    ones = lax.broadcasted_iota(jnp.int32, (16, 128), 0).astype(F32).astype(BF)

    def widen(p, _):
        wide[pl.ds(4 * p * ROWS, 4 * ROWS), :] = recv[pl.ds(4 * p, 4)].astype(F32).reshape(4 * ROWS, 128)
        return 0

    lax.fori_loop(0, 32, widen, 0)
    hi[...] = wide[pl.ds(SLOTS, 128, stride=ROWS), :].T
    lo[...] = wide[pl.ds(SLOTS + 1, 128, stride=ROWS), :].T

    def put(f, value):
        stack[f] = value
        for k in range(8):
            turned[pl.ds(f * BATCH + k, BATCH // 8, stride=8), :] = stack[f, pl.ds(7 - k, BATCH // 8, stride=8), :]

    put(0, bottom[...].astype(BF).astype(F32))
    turned[(F + 1) * BATCH :, :] = jnp.zeros(((31 - F) * BATCH, 128), F32)

    def hits(slot, keep=None):
        high = hi[pl.ds(slot, 1), :]
        if keep is not None:
            high = jnp.where(keep, high, 63.0)
        high = jnp.broadcast_to(high, (16, 128)).astype(BF)
        low = jnp.broadcast_to(lo[pl.ds(slot, 1), :], (16, 128)).astype(BF)
        low = jnp.where(low == ones, jnp.ones((), BF), zero)
        return jnp.concatenate([jnp.where(high == jnp.asarray(h, BF), low, zero) for h in range(32)], axis=0)

    def rows(slot):
        return wide[pl.ds(slot, 128, stride=ROWS), :].astype(BF)

    def pooled(g, places):
        for e in range(2):
            slots = [(FIXED * g + 2 * n + e, None) for n in range(3)]
            for at in places:
                keep = label[pl.ds(at, 1), :] == jnp.asarray(g, jnp.int32)
                slots.append((PERIOD * FIXED + 2 * at + e, keep))
            left = jnp.concatenate([hits(s, keep) for s, keep in slots], axis=1)
            right = jnp.concatenate([rows(s) for s, _ in slots], axis=0)
            total = jnp.dot(left, right, preferred_element_type=F32)
            put(1 + 2 * g + e, total.astype(BF).astype(F32))

    pooled(0, [0, 1, 2])

    def group(g, _):
        pooled(g, [lax.rem(g, 3)])
        return 0

    lax.fori_loop(1, PERIOD, group, 0)

    packed[:, :128] = bottom[...].astype(BF)
    own = lax.broadcasted_iota(jnp.int32, (8, 128), 1) % 8 == 7 - lax.broadcasted_iota(jnp.int32, (8, 128), 0)

    def interact(m, _):
        halves = []
        for half in range(2):
            left = stack[:, pl.ds(16 * m + 8 * half, 8), :].reshape(8 * (F + 1), 128).astype(BF)
            right = [turned[pl.ds(j * BATCH + 16 * m + 8 * half, 8), :] for j in range(32)]
            right = jnp.concatenate(right, axis=0).astype(BF)
            gram = lax.dot_general(left, right, (((1,), (1,)), ((), ())), preferred_element_type=F32)
            columns = []
            for a in range(4):
                for tile in range(1 if a < 2 else 2):
                    total = None
                    for c in range(8):
                        i = 8 * a + c
                        if i > F or 16 * tile >= i:
                            continue
                        part = jnp.where(own, gram[8 * i : 8 * i + 8, 128 * tile : 128 * tile + 128], 0.0)
                        part = pltpu.roll(part, c, 1, stride=1, stride_axis=0)
                        total = part if total is None else total + part
                    columns.append(total)
            halves.append(jnp.concatenate(columns, axis=1))
        packed[pl.ds(pl.multiple_of(16 * m, 16), 16), 128:] = jnp.concatenate(halves, axis=0).astype(BF)
        return 0

    lax.fori_loop(0, BATCH // 16, interact, 0)

    for m in range(4):
        at = pl.ds(128 * m, 128)
        hidden = jnp.dot(packed[at, :], weights[...], preferred_element_type=F32)
        hidden = jnp.maximum(hidden + bias[...], 0.0).astype(BF)
        out = lax.dot_general(last[...], hidden, (((1,), (1,)), ((), ())), preferred_element_type=F32)
        logits[:, at] = out[:1] + last_bias[0]
    x = logits[...]
    soft = jnp.maximum(x, 0.0) + jnp.log1p(jnp.exp(-jnp.abs(x)))
    term = jnp.sum(soft - marks[...].astype(F32) * x)
    loss[...] = jnp.full(loss.shape, term, F32)


def tail(label, recv, bottom, weights, bias, last, last_bias, marks):
    return pl.pallas_call(
        tail_kernel,
        out_shape=(jax.ShapeDtypeStruct((1, BATCH), F32), jax.ShapeDtypeStruct((128, 1, 128), F32)),
        in_specs=[VMEM] * 6 + [SMEM, VMEM],
        out_specs=(VMEM, VMEM),
        scratch_shapes=[
            pltpu.VMEM((128 * ROWS, 128), F32),
            pltpu.VMEM((128, 128), F32),
            pltpu.VMEM((128, 128), F32),
            pltpu.VMEM((F + 1, BATCH, 128), F32),
            pltpu.VMEM((32 * BATCH, 128), F32),
            pltpu.VMEM((BATCH, QW), BF),
        ],
        compiler_params=pltpu.CompilerParams(vmem_limit_bytes=40 << 20),
        cost_estimate=pl.CostEstimate(flops=6 << 30, transcendentals=0, bytes_accessed=5 << 20),
    )(label, recv, bottom, weights, bias, last, last_bias, marks)


def labels_by_holder():
    label = np.full((8, 128), -1, np.int32)
    label[:3] = LABEL[np.arange(128) % PERIOD].T
    return label


def exchange(value, axes):
    return lax.all_to_all(value, axes, split_axis=0, concat_axis=0, tiled=True)


def per_device(
    resident_row_blocks,
    orphan_blocks,
    home_offsets,
    home_lengths,
    home_samples,
    orphan_offsets,
    orphan_lengths,
    orphan_samples,
    orphan_owner,
    dense_inputs,
    labels,
    bottom_first,
    bias_first,
    bottom_second,
    bias_second,
    bottom_third,
    bias_third,
    top_hidden,
    bias_hidden,
    top_logit,
    bias_logit,
):
    chips = lax.axis_size("chip")
    mine = lax.axis_index(ALL)
    outgoing = route(orphan_owner[:, 0], orphan_blocks, chips)
    rehomed = exchange(outgoing, "chip")
    tab = lax.dynamic_index_in_dim(jnp.asarray(TABLE), mine % PERIOD, 0, keepdims=False)
    pieces = pool(
        tab,
        resident_row_blocks,
        orphan_blocks,
        home_offsets.transpose(0, 2, 1),
        home_lengths,
        home_samples,
        orphan_offsets.transpose(0, 2, 1),
        orphan_lengths,
        orphan_samples,
    )
    arrived = exchange(pieces, ALL)
    first = jax.nn.relu(
        jnp.dot(dense_inputs, bottom_first, preferred_element_type=F32) + bias_first
    ).astype(BF)
    second = jax.nn.relu(
        jnp.dot(first, bottom_second, preferred_element_type=F32) + bias_second
    ).astype(BF)
    bottom = jax.nn.relu(jnp.dot(second, bottom_third, preferred_element_type=F32) + bias_third)
    padded = jnp.concatenate([top_hidden, jnp.zeros((1, top_hidden.shape[1]), BF)], axis=0)
    weights = jnp.take(padded, jnp.asarray(FEATURE_ROWS), axis=0)
    last = jnp.broadcast_to(top_logit.reshape(1, -1), (8, top_logit.shape[0]))
    logits, term = tail(
        jnp.asarray(labels_by_holder()),
        arrived,
        bottom,
        weights,
        bias_hidden[None, :],
        last,
        bias_logit,
        labels[None, :],
    )
    loss = jnp.sum(exchange(term, ALL)[:, 0, 0])
    return rehomed, logits[0], loss


def solution(mesh):
    split = P(ALL)
    return jax.shard_map(
        per_device,
        mesh=mesh,
        in_specs=(split,) * 11 + (P(),) * 10,
        out_specs=(split, split, P()),
        check_vma=False,
    )
```

```python
import functools

import jax
import jax.numpy as jnp
import numpy as np
from jax import lax
from jax.experimental import pallas as pl
from jax.experimental.pallas import tpu as pltpu
from jax.sharding import PartitionSpec as P

ALL = ("hst", "chip")
PERIOD = 13
HOME, ORPHAN = 48, 32
FIXED = 6
SLOTS = 84
ROWS = 88
F = 26
BATCH = 512
NONE = 1023
QW = 896
BF, F32 = jnp.bfloat16, jnp.float32
VMEM = pl.BlockSpec(memory_space=pltpu.VMEM)
SMEM = pl.BlockSpec(memory_space=pltpu.SMEM)


def slot_tables():
    table = np.full((PERIOD, 128), -1, np.int32)
    label = np.full((PERIOD, 3), -1, np.int32)
    for r in range(PERIOD):
        for g in range(PERIOD):
            k = (g - 11 * r) % PERIOD
            o = (g - 4 - 3 * r) % PERIOD
            for e in range(2):
                table[r, FIXED * g + e] = 2 * k + e
                if k + PERIOD < HOME // 2:
                    table[r, FIXED * g + 2 + e] = 2 * (k + PERIOD) + e
                table[r, FIXED * g + 4 + e] = 2 * o + e
        rest = [(PERIOD + i, (4 + 3 * r + i) % PERIOD) for i in range(3)]
        free = [0, 1, 2]
        for k, g in sorted(rest, key=lambda item: item[1] == 0):
            at = g % 3 if g % 3 in free else free[0]
            free.remove(at)
            label[r, at] = g
            for e in range(2):
                table[r, PERIOD * FIXED + 2 * at + e] = 2 * k + e
    for g in range(1, PERIOD):
        assert all(at == g % 3 for r in range(PERIOD) for at in range(3) if label[r, at] == g)
    return table, label


def feature_rows():
    rows = np.full((QW,), 479, np.int32)
    rows[:128] = np.arange(128)
    at = 128
    for a in range(4):
        for tile in range(1 if a < 2 else 2):
            for lane in range(128):
                turn = (lane - 7) % 128
                i, j = 8 * a + turn % 8, 16 * tile + turn // 8
                if j < i <= F:
                    rows[at + lane] = 128 + i * (i - 1) // 2 + j
            at += 128
    return rows


TABLE, LABEL = slot_tables()
FEATURE_ROWS = feature_rows()


def route_kernel(owner, orphans, out, count):
    slots = out.shape[0] // count.shape[0]

    def clear(c, _):
        count[c] = 0
        return 0

    lax.fori_loop(0, count.shape[0], clear, 0)
    out[...] = jnp.zeros_like(out)

    def place(i, _):
        o = owner[i]
        n = count[o]
        out[slots * o + n] = orphans[i]
        count[o] = n + 1
        return 0

    lax.fori_loop(0, orphans.shape[0], place, 0)


def route(orphan_owner, orphans, chips):
    return pl.pallas_call(
        route_kernel,
        out_shape=jax.ShapeDtypeStruct((2 * chips,) + orphans.shape[1:], BF),
        in_specs=[SMEM, VMEM],
        out_specs=VMEM,
        scratch_shapes=[pltpu.SMEM((chips,), jnp.int32)],
        compiler_params=pltpu.CompilerParams(vmem_limit_bytes=16 << 20),
        cost_estimate=pl.CostEstimate(flops=0, transcendentals=0, bytes_accessed=3 << 20),
    )(orphan_owner, orphans)


def pool_kernel(*refs):
    given, out, (wide, sam), held, sem = refs[:8], refs[8], refs[9:11], refs[11:19], refs[19]
    copies = [pltpu.make_async_copy(g, h, sem.at[n]) for n, (g, h) in enumerate(zip(given, held))]
    for copy in copies:
        copy.start()
    home, orphan = (held[0],) + tuple(held[2:5]), (held[1],) + tuple(held[5:8])
    me = lax.axis_index("hst") * lax.axis_size("chip") + lax.axis_index("chip")
    rows = lax.broadcasted_iota(jnp.int32, (128, 128), 0).astype(F32).astype(BF)
    place = lax.broadcasted_iota(jnp.int32, (8, 128), 0)
    one, zero = jnp.ones((), BF), jnp.zeros((), BF)
    sam[...] = jnp.full(sam.shape, NONE, jnp.int32)
    for s in range(SLOTS + 2, ROWS):
        wide[pl.ds(s, 128, stride=ROWS), :] = jnp.zeros((128, 128), F32)
    for copy in copies:
        copy.wait()

    def piece(slot, b, blocks, off, length, samples):
        live = jnp.where(place < length[pl.ds(b, 1), :], off[b], -1).astype(F32).astype(BF)
        counts = jnp.zeros((128, 128), BF)
        for n in range(8):
            counts = counts + jnp.where(rows == live[n : n + 1, :], one, zero)
        sums = lax.dot_general(counts, blocks[b], (((0,), (0,)), ((), ())), preferred_element_type=F32)
        wide[pl.ds(slot, 128, stride=ROWS), :] = sums
        sam[pl.ds(slot, 1), :] = samples[pl.ds(b, 1), :]

    def pair(k, more):
        g = FIXED * lax.rem(11 * me + k, PERIOD)
        for e in range(2):
            piece(g + e, 2 * k + e, *home)
        for e in range(2):
            if more:
                piece(g + 2 + e, 2 * (k + PERIOD) + e, *home)
            else:
                wide[pl.ds(g + 2 + e, 128, stride=ROWS), :] = jnp.zeros((128, 128), F32)
        g = FIXED * lax.rem(4 + 3 * me + k, PERIOD)
        for e in range(2):
            piece(g + 4 + e, 2 * k + e, *orphan)

    def step(k, _):
        pair(k, True)
        return 0

    both = HOME // 2 - PERIOD
    lax.fori_loop(0, both, step, 0, unroll=2)
    for k in range(both, PERIOD):
        pair(k, False)
    rest = [lax.rem(4 + 3 * me + i, PERIOD) for i in range(3)]
    for i, g in enumerate(rest):
        others = sum(lax.rem(h, 3) for h in rest if h is not g)
        at = jnp.where(g == 0, 3 - others, lax.rem(g, 3))
        for e in range(2):
            piece(PERIOD * FIXED + 2 * at + e, 2 * (PERIOD + i) + e, *orphan)
    index = sam[...]
    wide[pl.ds(SLOTS, 128, stride=ROWS), :] = (index >> 4).astype(F32).T
    wide[pl.ds(SLOTS + 1, 128, stride=ROWS), :] = (index & 15).astype(F32).T

    def narrow(q, _):
        out[pl.ds(4 * q, 4)] = wide[pl.ds(4 * q * ROWS, 4 * ROWS), :].reshape(4, ROWS, 128).astype(BF)
        return 0

    lax.fori_loop(0, 32, narrow, 0, unroll=2)


def pool(*arrays):
    return pl.pallas_call(
        pool_kernel,
        out_shape=jax.ShapeDtypeStruct((128, ROWS, 128), BF),
        in_specs=[pl.BlockSpec(memory_space=pl.ANY)] * 8,
        out_specs=VMEM,
        scratch_shapes=[pltpu.VMEM((128 * ROWS, 128), F32), pltpu.VMEM((128, 128), jnp.int32)]
        + [pltpu.VMEM(a.shape, a.dtype) for a in arrays]
        + [pltpu.SemaphoreType.DMA((8,))],
        compiler_params=pltpu.CompilerParams(vmem_limit_bytes=24 << 20),
        cost_estimate=pl.CostEstimate(flops=84 * 128 * 128 * 256, transcendentals=0, bytes_accessed=6 << 20),
    )(*arrays)


def tail_kernel(label, recv, bottom, weights, bias, last, last_bias, marks, logits, loss, wide, hi, lo, stack, turned, packed):
    zero = jnp.zeros((), BF)
    ones = lax.broadcasted_iota(jnp.int32, (16, 128), 0).astype(F32).astype(BF)

    def widen(p, _):
        wide[pl.ds(4 * p * ROWS, 4 * ROWS), :] = recv[pl.ds(4 * p, 4)].astype(F32).reshape(4 * ROWS, 128)
        return 0

    lax.fori_loop(0, 32, widen, 0, unroll=2)
    hi[...] = wide[pl.ds(SLOTS, 128, stride=ROWS), :].T
    lo[...] = wide[pl.ds(SLOTS + 1, 128, stride=ROWS), :].T

    def put(f, value):
        stack[f] = value
        for k in range(8):
            turned[pl.ds(f * BATCH + k, BATCH // 8, stride=8), :] = stack[f, pl.ds(7 - k, BATCH // 8, stride=8), :]

    put(0, bottom[...].astype(BF).astype(F32))
    turned[(F + 1) * BATCH :, :] = jnp.zeros(((31 - F) * BATCH, 128), F32)

    def hits(slot, keep=None):
        high = hi[pl.ds(slot, 1), :]
        if keep is not None:
            high = jnp.where(keep, high, 63.0)
        high = jnp.broadcast_to(high, (16, 128)).astype(BF)
        low = jnp.broadcast_to(lo[pl.ds(slot, 1), :], (16, 128)).astype(BF)
        low = jnp.where(low == ones, jnp.ones((), BF), zero)
        return jnp.concatenate([jnp.where(high == jnp.asarray(h, BF), low, zero) for h in range(32)], axis=0)

    def rows(slot):
        return wide[pl.ds(slot, 128, stride=ROWS), :].astype(BF)

    def pooled(g, places):
        for e in range(2):
            slots = [(FIXED * g + 2 * n + e, None) for n in range(3)]
            for at in places:
                keep = label[pl.ds(at, 1), :] == jnp.asarray(g, jnp.int32)
                slots.append((PERIOD * FIXED + 2 * at + e, keep))
            left = jnp.concatenate([hits(s, keep) for s, keep in slots], axis=1)
            right = jnp.concatenate([rows(s) for s, _ in slots], axis=0)
            total = jnp.dot(left, right, preferred_element_type=F32)
            put(1 + 2 * g + e, total.astype(BF).astype(F32))

    pooled(0, [0, 1, 2])

    def group(g, _):
        pooled(g, [lax.rem(g, 3)])
        return 0

    lax.fori_loop(1, PERIOD, group, 0, unroll=4)

    packed[:, :128] = bottom[...].astype(BF)
    own = lax.broadcasted_iota(jnp.int32, (8, 128), 1) % 8 == 7 - lax.broadcasted_iota(jnp.int32, (8, 128), 0)

    def interact(m, _):
        halves = []
        for half in range(2):
            left = stack[:, pl.ds(16 * m + 8 * half, 8), :].reshape(8 * (F + 1), 128).astype(BF)
            right = [turned[pl.ds(j * BATCH + 16 * m + 8 * half, 8), :] for j in range(32)]
            right = jnp.concatenate(right, axis=0).astype(BF)
            gram = lax.dot_general(left, right, (((1,), (1,)), ((), ())), preferred_element_type=F32)
            columns = []
            for a in range(4):
                for tile in range(1 if a < 2 else 2):
                    total = None
                    for c in range(8):
                        i = 8 * a + c
                        if i > F or 16 * tile >= i:
                            continue
                        part = jnp.where(own, gram[8 * i : 8 * i + 8, 128 * tile : 128 * tile + 128], 0.0)
                        part = pltpu.roll(part, c, 1, stride=1, stride_axis=0)
                        total = part if total is None else total + part
                    columns.append(total)
            halves.append(jnp.concatenate(columns, axis=1))
        packed[pl.ds(pl.multiple_of(16 * m, 16), 16), 128:] = jnp.concatenate(halves, axis=0).astype(BF)
        return 0

    lax.fori_loop(0, BATCH // 16, interact, 0, unroll=4)

    for m in range(4):
        at = pl.ds(128 * m, 128)
        hidden = jnp.dot(packed[at, :], weights[...], preferred_element_type=F32)
        hidden = jnp.maximum(hidden + bias[...], 0.0).astype(BF)
        out = lax.dot_general(last[...], hidden, (((1,), (1,)), ((), ())), preferred_element_type=F32)
        logits[:, at] = out[:1] + last_bias[0]
    x = logits[...]
    soft = jnp.maximum(x, 0.0) + jnp.log1p(jnp.exp(-jnp.abs(x)))
    term = jnp.sum(soft - marks[...].astype(F32) * x)
    loss[...] = jnp.full(loss.shape, term, F32)


def tail(label, recv, bottom, weights, bias, last, last_bias, marks):
    return pl.pallas_call(
        tail_kernel,
        out_shape=(jax.ShapeDtypeStruct((1, BATCH), F32), jax.ShapeDtypeStruct((1, 128), F32)),
        in_specs=[VMEM] * 6 + [SMEM, VMEM],
        out_specs=(VMEM, VMEM),
        scratch_shapes=[
            pltpu.VMEM((128 * ROWS, 128), F32),
            pltpu.VMEM((128, 128), F32),
            pltpu.VMEM((128, 128), F32),
            pltpu.VMEM((F + 1, BATCH, 128), F32),
            pltpu.VMEM((32 * BATCH, 128), F32),
            pltpu.VMEM((BATCH, QW), BF),
        ],
        compiler_params=pltpu.CompilerParams(vmem_limit_bytes=40 << 20),
        cost_estimate=pl.CostEstimate(flops=6 << 30, transcendentals=0, bytes_accessed=5 << 20),
    )(label, recv, bottom, weights, bias, last, last_bias, marks)


def labels_by_holder():
    label = np.full((8, 128), -1, np.int32)
    label[:3] = LABEL[np.arange(128) % PERIOD].T
    return label


def exchange(value, axes):
    return lax.all_to_all(value, axes, split_axis=0, concat_axis=0, tiled=True)


def ring_sum(value, axis, size, step):
    def shifted(k):
        pairs = [(i, i - i // step % 4 * step + (i // step + k) % 4 * step) for i in range(size)]
        return lax.ppermute(value, axis, pairs)

    return (value + shifted(2)) + (shifted(1) + shifted(3))


def per_device(
    resident_row_blocks,
    orphan_blocks,
    home_offsets,
    home_lengths,
    home_samples,
    orphan_offsets,
    orphan_lengths,
    orphan_samples,
    orphan_owner,
    dense_inputs,
    labels,
    bottom_first,
    bias_first,
    bottom_second,
    bias_second,
    bottom_third,
    bias_third,
    top_hidden,
    bias_hidden,
    top_logit,
    bias_logit,
):
    chips = lax.axis_size("chip")
    outgoing = route(orphan_owner[:, 0], orphan_blocks, chips)
    pieces = pool(
        resident_row_blocks,
        orphan_blocks,
        home_offsets.transpose(0, 2, 1),
        home_lengths,
        home_samples,
        orphan_offsets.transpose(0, 2, 1),
        orphan_lengths,
        orphan_samples,
    )
    arrived = exchange(pieces, ALL)
    first = jax.nn.relu(
        jnp.dot(dense_inputs, bottom_first, preferred_element_type=F32) + bias_first
    ).astype(BF)
    second = jax.nn.relu(
        jnp.dot(first, bottom_second, preferred_element_type=F32) + bias_second
    ).astype(BF)
    bottom = jax.nn.relu(jnp.dot(second, bottom_third, preferred_element_type=F32) + bias_third)
    padded = jnp.concatenate([top_hidden, jnp.zeros((1, top_hidden.shape[1]), BF)], axis=0)
    weights = jnp.take(padded, jnp.asarray(FEATURE_ROWS), axis=0)
    last = jnp.broadcast_to(top_logit.reshape(1, -1), (8, top_logit.shape[0]))
    outgoing, weights, bottom, last = lax.optimization_barrier((outgoing, weights, bottom, last))
    rehomed = exchange(outgoing, "chip")
    logits, term = tail(
        jnp.asarray(labels_by_holder()),
        arrived,
        bottom,
        weights,
        bias_hidden[None, :],
        last,
        bias_logit,
        labels[None, :],
    )
    term = ring_sum(term, "hst", lax.axis_size("hst"), 1)
    term = term + lax.ppermute(term, "chip", [(i, i ^ 1) for i in range(chips)])
    term = ring_sum(term, "chip", chips, 2)
    term = ring_sum(term, "chip", chips, 8)
    return rehomed, logits[0], term[0, 0]


def solution(mesh):
    split = P(ALL)
    return jax.shard_map(
        per_device,
        mesh=mesh,
        in_specs=(split,) * 11 + (P(),) * 10,
        out_specs=(split, split, P()),
        check_vma=False,
    )
```

```python
import functools

import jax
import jax.numpy as jnp
import numpy as np
from jax import lax
from jax.experimental import pallas as pl
from jax.experimental.pallas import tpu as pltpu
from jax.sharding import PartitionSpec as P

ALL = ("hst", "chip")
PERIOD = 13
HOME, ORPHAN = 48, 32
FIXED = 6
SLOTS = 84
ROWS = 88
F = 26
BATCH = 512
NONE = 1023
QW = 896
BF, F32 = jnp.bfloat16, jnp.float32
VMEM = pl.BlockSpec(memory_space=pltpu.VMEM)
SMEM = pl.BlockSpec(memory_space=pltpu.SMEM)


def slot_tables():
    table = np.full((PERIOD, 128), -1, np.int32)
    label = np.full((PERIOD, 3), -1, np.int32)
    for r in range(PERIOD):
        for g in range(PERIOD):
            k = (g - 11 * r) % PERIOD
            o = (g - 4 - 3 * r) % PERIOD
            for e in range(2):
                table[r, FIXED * g + e] = 2 * k + e
                if k + PERIOD < HOME // 2:
                    table[r, FIXED * g + 2 + e] = 2 * (k + PERIOD) + e
                table[r, FIXED * g + 4 + e] = 2 * o + e
        rest = [(PERIOD + i, (4 + 3 * r + i) % PERIOD) for i in range(3)]
        free = [0, 1, 2]
        for k, g in sorted(rest, key=lambda item: item[1] == 0):
            at = g % 3 if g % 3 in free else free[0]
            free.remove(at)
            label[r, at] = g
            for e in range(2):
                table[r, PERIOD * FIXED + 2 * at + e] = 2 * k + e
    for g in range(1, PERIOD):
        assert all(at == g % 3 for r in range(PERIOD) for at in range(3) if label[r, at] == g)
    return table, label


def feature_rows():
    rows = np.full((QW,), 479, np.int32)
    rows[:128] = np.arange(128)
    at = 128
    for a in range(4):
        for tile in range(1 if a < 2 else 2):
            for lane in range(128):
                turn = (lane - 7) % 128
                i, j = 8 * a + turn % 8, 16 * tile + turn // 8
                if j < i <= F:
                    rows[at + lane] = 128 + i * (i - 1) // 2 + j
            at += 128
    return rows


TABLE, LABEL = slot_tables()
FEATURE_ROWS = feature_rows()


def route_kernel(owner, orphans, out, count):
    slots = out.shape[0] // count.shape[0]

    def clear(c, _):
        count[c] = 0
        return 0

    lax.fori_loop(0, count.shape[0], clear, 0)
    out[...] = jnp.zeros_like(out)

    def place(i, _):
        o = owner[i]
        n = count[o]
        out[slots * o + n] = orphans[i]
        count[o] = n + 1
        return 0

    lax.fori_loop(0, orphans.shape[0], place, 0)


def route(orphan_owner, orphans, chips):
    return pl.pallas_call(
        route_kernel,
        out_shape=jax.ShapeDtypeStruct((2 * chips,) + orphans.shape[1:], BF),
        in_specs=[SMEM, VMEM],
        out_specs=VMEM,
        scratch_shapes=[pltpu.SMEM((chips,), jnp.int32)],
        compiler_params=pltpu.CompilerParams(vmem_limit_bytes=16 << 20),
        cost_estimate=pl.CostEstimate(flops=0, transcendentals=0, bytes_accessed=3 << 20),
    )(orphan_owner, orphans)


def pool_kernel(*refs):
    given, out, (wide, sam), held, sem = refs[:8], refs[8], refs[9:11], refs[11:19], refs[19]
    copies = [pltpu.make_async_copy(g, h, sem.at[n]) for n, (g, h) in enumerate(zip(given, held))]
    for copy in copies:
        copy.start()
    home, orphan = (held[0],) + tuple(held[2:5]), (held[1],) + tuple(held[5:8])
    me = lax.axis_index("hst") * lax.axis_size("chip") + lax.axis_index("chip")
    rows = lax.broadcasted_iota(jnp.int32, (128, 128), 0).astype(F32).astype(BF)
    place = lax.broadcasted_iota(jnp.int32, (8, 128), 0)
    one, zero = jnp.ones((), BF), jnp.zeros((), BF)
    sam[...] = jnp.full(sam.shape, NONE, jnp.int32)
    for s in range(SLOTS + 2, ROWS):
        wide[pl.ds(s, 128, stride=ROWS), :] = jnp.zeros((128, 128), F32)
    for copy in copies:
        copy.wait()

    def piece(slot, b, blocks, off, length, samples):
        live = jnp.where(place < length[pl.ds(b, 1), :], off[b], -1).astype(F32).astype(BF)
        counts = jnp.zeros((128, 128), BF)
        for n in range(8):
            counts = counts + jnp.where(rows == live[n : n + 1, :], one, zero)
        sums = lax.dot_general(counts, blocks[b], (((0,), (0,)), ((), ())), preferred_element_type=F32)
        wide[pl.ds(slot, 128, stride=ROWS), :] = sums
        sam[pl.ds(slot, 1), :] = samples[pl.ds(b, 1), :]

    def pair(k, more):
        g = FIXED * lax.rem(11 * me + k, PERIOD)
        for e in range(2):
            piece(g + e, 2 * k + e, *home)
        for e in range(2):
            if more:
                piece(g + 2 + e, 2 * (k + PERIOD) + e, *home)
            else:
                wide[pl.ds(g + 2 + e, 128, stride=ROWS), :] = jnp.zeros((128, 128), F32)
        g = FIXED * lax.rem(4 + 3 * me + k, PERIOD)
        for e in range(2):
            piece(g + 4 + e, 2 * k + e, *orphan)

    def step(k, _):
        pair(k, True)
        return 0

    both = HOME // 2 - PERIOD
    lax.fori_loop(0, both, step, 0, unroll=2)
    for k in range(both, PERIOD):
        pair(k, False)
    rest = [lax.rem(4 + 3 * me + i, PERIOD) for i in range(3)]
    for i, g in enumerate(rest):
        others = sum(lax.rem(h, 3) for h in rest if h is not g)
        at = jnp.where(g == 0, 3 - others, lax.rem(g, 3))
        for e in range(2):
            piece(PERIOD * FIXED + 2 * at + e, 2 * (PERIOD + i) + e, *orphan)
    index = sam[...]
    wide[pl.ds(SLOTS, 128, stride=ROWS), :] = (index >> 4).astype(F32).T
    wide[pl.ds(SLOTS + 1, 128, stride=ROWS), :] = (index & 15).astype(F32).T

    def narrow(q, _):
        out[pl.ds(4 * q, 4)] = wide[pl.ds(4 * q * ROWS, 4 * ROWS), :].reshape(4, ROWS, 128).astype(BF)
        return 0

    lax.fori_loop(0, 32, narrow, 0, unroll=2)


def pool(*arrays):
    return pl.pallas_call(
        pool_kernel,
        out_shape=jax.ShapeDtypeStruct((128, ROWS, 128), BF),
        in_specs=[pl.BlockSpec(memory_space=pl.ANY)] * 8,
        out_specs=VMEM,
        scratch_shapes=[pltpu.VMEM((128 * ROWS, 128), F32), pltpu.VMEM((128, 128), jnp.int32)]
        + [pltpu.VMEM(a.shape, a.dtype) for a in arrays]
        + [pltpu.SemaphoreType.DMA((8,))],
        compiler_params=pltpu.CompilerParams(vmem_limit_bytes=60 << 20),
        cost_estimate=pl.CostEstimate(flops=84 * 128 * 128 * 256, transcendentals=0, bytes_accessed=6 << 20),
    )(*arrays)


def tail_kernel(label, recv, bottom, weights, bias, last, last_bias, marks, logits, loss, wide, hi, lo, stack, turned, packed):
    zero = jnp.zeros((), BF)
    ones = lax.broadcasted_iota(jnp.int32, (16, 128), 0).astype(F32).astype(BF)

    def widen(p, _):
        wide[pl.ds(4 * p * ROWS, 4 * ROWS), :] = recv[pl.ds(4 * p, 4)].astype(F32).reshape(4 * ROWS, 128)
        return 0

    lax.fori_loop(0, 32, widen, 0, unroll=2)
    hi[...] = wide[pl.ds(SLOTS, 128, stride=ROWS), :].T
    lo[...] = wide[pl.ds(SLOTS + 1, 128, stride=ROWS), :].T

    def put(f, value):
        stack[f] = value
        for k in range(8):
            turned[pl.ds(f * BATCH + k, BATCH // 8, stride=8), :] = stack[f, pl.ds(7 - k, BATCH // 8, stride=8), :]

    put(0, bottom[...].astype(BF).astype(F32))
    turned[(F + 1) * BATCH :, :] = jnp.zeros(((31 - F) * BATCH, 128), F32)

    def hits(slot, keep=None):
        high = hi[pl.ds(slot, 1), :]
        if keep is not None:
            high = jnp.where(keep, high, 63.0)
        high = jnp.broadcast_to(high, (16, 128)).astype(BF)
        low = jnp.broadcast_to(lo[pl.ds(slot, 1), :], (16, 128)).astype(BF)
        low = jnp.where(low == ones, jnp.ones((), BF), zero)
        return jnp.concatenate([jnp.where(high == jnp.asarray(h, BF), low, zero) for h in range(32)], axis=0)

    def rows(slot):
        return wide[pl.ds(slot, 128, stride=ROWS), :].astype(BF)

    def pooled(g, places):
        for e in range(2):
            slots = [(FIXED * g + 2 * n + e, None) for n in range(3)]
            for at in places:
                keep = label[pl.ds(at, 1), :] == jnp.asarray(g, jnp.int32)
                slots.append((PERIOD * FIXED + 2 * at + e, keep))
            left = jnp.concatenate([hits(s, keep) for s, keep in slots], axis=1)
            right = jnp.concatenate([rows(s) for s, _ in slots], axis=0)
            total = jnp.dot(left, right, preferred_element_type=F32)
            put(1 + 2 * g + e, total.astype(BF).astype(F32))

    pooled(0, [0, 1, 2])

    def group(g, _):
        pooled(g, [lax.rem(g, 3)])
        return 0

    lax.fori_loop(1, PERIOD, group, 0, unroll=4)

    packed[:, :128] = bottom[...].astype(BF)
    own = lax.broadcasted_iota(jnp.int32, (8, 128), 1) % 8 == 7 - lax.broadcasted_iota(jnp.int32, (8, 128), 0)

    def interact(m, _):
        halves = []
        for half in range(2):
            left = stack[:, pl.ds(16 * m + 8 * half, 8), :].reshape(8 * (F + 1), 128).astype(BF)
            right = [turned[pl.ds(j * BATCH + 16 * m + 8 * half, 8), :] for j in range(32)]
            right = jnp.concatenate(right, axis=0).astype(BF)
            gram = lax.dot_general(left, right, (((1,), (1,)), ((), ())), preferred_element_type=F32)
            columns = []
            for a in range(4):
                for tile in range(1 if a < 2 else 2):
                    total = None
                    for c in range(8):
                        i = 8 * a + c
                        if i > F or 16 * tile >= i:
                            continue
                        part = jnp.where(own, gram[8 * i : 8 * i + 8, 128 * tile : 128 * tile + 128], 0.0)
                        part = pltpu.roll(part, c, 1, stride=1, stride_axis=0)
                        total = part if total is None else total + part
                    columns.append(total)
            halves.append(jnp.concatenate(columns, axis=1))
        packed[pl.ds(pl.multiple_of(16 * m, 16), 16), 128:] = jnp.concatenate(halves, axis=0).astype(BF)
        return 0

    lax.fori_loop(0, BATCH // 16, interact, 0, unroll=4)

    for m in range(4):
        at = pl.ds(128 * m, 128)
        hidden = jnp.dot(packed[at, :], weights[...], preferred_element_type=F32)
        hidden = jnp.maximum(hidden + bias[...], 0.0).astype(BF)
        out = lax.dot_general(last[...], hidden, (((1,), (1,)), ((), ())), preferred_element_type=F32)
        logits[:, at] = out[:1] + last_bias[0]
    x = logits[...]
    soft = jnp.maximum(x, 0.0) + jnp.log1p(jnp.exp(-jnp.abs(x)))
    term = jnp.sum(soft - marks[...].astype(F32) * x)
    loss[...] = jnp.full(loss.shape, term, F32)


def tail(label, recv, bottom, weights, bias, last, last_bias, marks):
    return pl.pallas_call(
        tail_kernel,
        out_shape=(jax.ShapeDtypeStruct((1, BATCH), F32), jax.ShapeDtypeStruct((1, 128), F32)),
        in_specs=[VMEM] * 6 + [SMEM, VMEM],
        out_specs=(VMEM, VMEM),
        scratch_shapes=[
            pltpu.VMEM((128 * ROWS, 128), F32),
            pltpu.VMEM((128, 128), F32),
            pltpu.VMEM((128, 128), F32),
            pltpu.VMEM((F + 1, BATCH, 128), F32),
            pltpu.VMEM((32 * BATCH, 128), F32),
            pltpu.VMEM((BATCH, QW), BF),
        ],
        compiler_params=pltpu.CompilerParams(vmem_limit_bytes=40 << 20),
        cost_estimate=pl.CostEstimate(flops=6 << 30, transcendentals=0, bytes_accessed=5 << 20),
    )(label, recv, bottom, weights, bias, last, last_bias, marks)


def labels_by_holder():
    label = np.full((8, 128), -1, np.int32)
    label[:3] = LABEL[np.arange(128) % PERIOD].T
    return label


def exchange(value, axes):
    return lax.all_to_all(value, axes, split_axis=0, concat_axis=0, tiled=True)


def ring_sum(value, axis, size, step):
    for other in ((1, 0, 3, 2), (3, 2, 1, 0)):
        pairs = [(i, i + (other[i // step % 4] - i // step % 4) * step) for i in range(size)]
        value = value + lax.ppermute(value, axis, pairs)
    return value


def keep_kernel(given, out, sems):
    part = given.shape[0] // sems.shape[0]
    copies = []
    for n in range(sems.shape[0]):
        at = pl.ds(n * part, part)
        copies.append(pltpu.make_async_copy(given.at[at], out.at[at], sems.at[n]))
    for copy in copies:
        copy.start()
    for copy in copies:
        copy.wait()


def keep(value):
    return pl.pallas_call(
        keep_kernel,
        out_shape=jax.ShapeDtypeStruct(value.shape, value.dtype),
        in_specs=[pl.BlockSpec(memory_space=pl.ANY)],
        out_specs=pl.BlockSpec(memory_space=pl.ANY),
        scratch_shapes=[pltpu.SemaphoreType.DMA((8,))],
        compiler_params=pltpu.CompilerParams(vmem_limit_bytes=60 << 20),
        cost_estimate=pl.CostEstimate(flops=0, transcendentals=0, bytes_accessed=4 << 20),
    )(value)


def per_device(
    resident_row_blocks,
    orphan_blocks,
    home_offsets,
    home_lengths,
    home_samples,
    orphan_offsets,
    orphan_lengths,
    orphan_samples,
    orphan_owner,
    dense_inputs,
    labels,
    bottom_first,
    bias_first,
    bottom_second,
    bias_second,
    bottom_third,
    bias_third,
    top_hidden,
    bias_hidden,
    top_logit,
    bias_logit,
):
    chips = lax.axis_size("chip")
    outgoing = route(orphan_owner[:, 0], orphan_blocks, chips)
    pieces = pool(
        resident_row_blocks,
        orphan_blocks,
        home_offsets.transpose(0, 2, 1),
        home_lengths,
        home_samples,
        orphan_offsets.transpose(0, 2, 1),
        orphan_lengths,
        orphan_samples,
    )
    arrived = exchange(pieces, ALL)
    first = jax.nn.relu(
        jnp.dot(dense_inputs, bottom_first, preferred_element_type=F32) + bias_first
    ).astype(BF)
    second = jax.nn.relu(
        jnp.dot(first, bottom_second, preferred_element_type=F32) + bias_second
    ).astype(BF)
    bottom = jax.nn.relu(jnp.dot(second, bottom_third, preferred_element_type=F32) + bias_third)
    padded = jnp.concatenate([top_hidden, jnp.zeros((1, top_hidden.shape[1]), BF)], axis=0)
    weights = jnp.take(padded, jnp.asarray(FEATURE_ROWS), axis=0)
    last = jnp.broadcast_to(top_logit.reshape(1, -1), (8, top_logit.shape[0]))
    outgoing, weights, bottom, last = lax.optimization_barrier((outgoing, weights, bottom, last))
    rehomed = exchange(outgoing, "chip")
    logits, term = tail(
        jnp.asarray(labels_by_holder()),
        arrived,
        bottom,
        weights,
        bias_hidden[None, :],
        last,
        bias_logit,
        labels[None, :],
    )
    term = ring_sum(term, "hst", lax.axis_size("hst"), 1)
    term = term + lax.ppermute(term, "chip", [(i, i ^ 1) for i in range(chips)])
    term = ring_sum(term, "chip", chips, 2)
    rehomed, term = lax.optimization_barrier((keep(rehomed), term))
    term = ring_sum(term, "chip", chips, 8)
    return rehomed, logits[0], term[0, 0]


def solution(mesh):
    split = P(ALL)
    return jax.shard_map(
        per_device,
        mesh=mesh,
        in_specs=(split,) * 11 + (P(),) * 10,
        out_specs=(split, split, P()),
        check_vma=False,
    )
```

```python
import functools

import jax
import jax.numpy as jnp
import numpy as np
from jax import lax
from jax.experimental import pallas as pl
from jax.experimental.pallas import tpu as pltpu
from jax.sharding import PartitionSpec as P

ALL = ("hst", "chip")
PERIOD = 13
HOME, ORPHAN = 48, 32
FIXED = 6
SLOTS = 84
ROWS = 88
F = 26
BATCH = 512
NONE = 1023
QW = 896
BF, F32 = jnp.bfloat16, jnp.float32
VMEM = pl.BlockSpec(memory_space=pltpu.VMEM)
SMEM = pl.BlockSpec(memory_space=pltpu.SMEM)


def slot_tables():
    table = np.full((PERIOD, 128), -1, np.int32)
    label = np.full((PERIOD, 3), -1, np.int32)
    for r in range(PERIOD):
        for g in range(PERIOD):
            k = (g - 11 * r) % PERIOD
            o = (g - 4 - 3 * r) % PERIOD
            for e in range(2):
                table[r, FIXED * g + e] = 2 * k + e
                if k + PERIOD < HOME // 2:
                    table[r, FIXED * g + 2 + e] = 2 * (k + PERIOD) + e
                table[r, FIXED * g + 4 + e] = 2 * o + e
        rest = [(PERIOD + i, (4 + 3 * r + i) % PERIOD) for i in range(3)]
        free = [0, 1, 2]
        for k, g in sorted(rest, key=lambda item: item[1] == 0):
            at = g % 3 if g % 3 in free else free[0]
            free.remove(at)
            label[r, at] = g
            for e in range(2):
                table[r, PERIOD * FIXED + 2 * at + e] = 2 * k + e
    for g in range(1, PERIOD):
        assert all(at == g % 3 for r in range(PERIOD) for at in range(3) if label[r, at] == g)
    return table, label


def feature_rows():
    rows = np.full((QW,), 479, np.int32)
    rows[:128] = np.arange(128)
    at = 128
    for a in range(4):
        for tile in range(1 if a < 2 else 2):
            for lane in range(128):
                turn = (lane - 7) % 128
                i, j = 8 * a + turn % 8, 16 * tile + turn // 8
                if j < i <= F:
                    rows[at + lane] = 128 + i * (i - 1) // 2 + j
            at += 128
    return rows


TABLE, LABEL = slot_tables()
FEATURE_ROWS = feature_rows()


def route_kernel(owner, orphans, out, count):
    slots = out.shape[0] // count.shape[0]

    def clear(c, _):
        count[c] = 0
        return 0

    lax.fori_loop(0, count.shape[0], clear, 0)
    out[...] = jnp.zeros_like(out)

    def place(i, _):
        o = owner[i]
        n = count[o]
        out[slots * o + n] = orphans[i]
        count[o] = n + 1
        return 0

    lax.fori_loop(0, orphans.shape[0], place, 0)


def route(orphan_owner, orphans, chips):
    return pl.pallas_call(
        route_kernel,
        out_shape=jax.ShapeDtypeStruct((2 * chips,) + orphans.shape[1:], BF),
        in_specs=[SMEM, VMEM],
        out_specs=VMEM,
        scratch_shapes=[pltpu.SMEM((chips,), jnp.int32)],
        compiler_params=pltpu.CompilerParams(vmem_limit_bytes=16 << 20),
        cost_estimate=pl.CostEstimate(flops=0, transcendentals=0, bytes_accessed=3 << 20),
    )(orphan_owner, orphans)


def pool_kernel(*refs):
    given, out, (wide, sam, ready), held, sem, sent = refs[:8], refs[8], refs[9:12], refs[12:20], refs[20], refs[21]
    cuts = [(n, None) for n in range(2, 8)] + [(0, (0, 12)), (0, (26, 38)), (1, (0, 12))]
    cuts = [cuts, [(0, (12, 26)), (0, (38, 48)), (1, (12, 32))]]
    waves = []
    for wave in cuts:
        copies = []
        for n, cut in wave:
            at = pl.ds(cut[0], cut[1] - cut[0]) if cut else pl.ds(0, given[n].shape[0])
            number = len(copies) + 9 * len(waves)
            copies.append(pltpu.make_async_copy(given[n].at[at], held[n].at[at], sem.at[number]))
            copies[-1].start()
        waves.append(copies)
    home, orphan = (held[0],) + tuple(held[2:5]), (held[1],) + tuple(held[5:8])
    me = lax.axis_index("hst") * lax.axis_size("chip") + lax.axis_index("chip")
    rows = lax.broadcasted_iota(jnp.int32, (128, 128), 0).astype(F32).astype(BF)
    place = lax.broadcasted_iota(jnp.int32, (8, 128), 0)
    one, zero = jnp.ones((), BF), jnp.zeros((), BF)
    sam[...] = jnp.full(sam.shape, NONE, jnp.int32)
    for s in range(SLOTS + 2, ROWS):
        wide[pl.ds(s, 128, stride=ROWS), :] = jnp.zeros((128, 128), F32)
    for copy in waves[0]:
        copy.wait()

    def piece(slot, b, blocks, off, length, samples):
        live = jnp.where(place < length[pl.ds(b, 1), :], off[b], -1).astype(F32).astype(BF)
        counts = jnp.zeros((128, 128), BF)
        for n in range(8):
            counts = counts + jnp.where(rows == live[n : n + 1, :], one, zero)
        sums = lax.dot_general(counts, blocks[b], (((0,), (0,)), ((), ())), preferred_element_type=F32)
        wide[pl.ds(slot, 128, stride=ROWS), :] = sums
        sam[pl.ds(slot, 1), :] = samples[pl.ds(b, 1), :]

    def pair(k, more):
        g = FIXED * lax.rem(11 * me + k, PERIOD)
        for e in range(2):
            piece(g + e, 2 * k + e, *home)
        for e in range(2):
            if more:
                piece(g + 2 + e, 2 * (k + PERIOD) + e, *home)
            else:
                wide[pl.ds(g + 2 + e, 128, stride=ROWS), :] = jnp.zeros((128, 128), F32)
        g = FIXED * lax.rem(4 + 3 * me + k, PERIOD)
        for e in range(2):
            piece(g + 4 + e, 2 * k + e, *orphan)

    def step(k, _):
        pair(k, True)
        return 0

    both = HOME // 2 - PERIOD
    lax.fori_loop(0, 6, step, 0, unroll=3)
    for copy in waves[1]:
        copy.wait()
    lax.fori_loop(6, both, step, 0, unroll=5)
    for k in range(both, PERIOD):
        pair(k, False)
    rest = [lax.rem(4 + 3 * me + i, PERIOD) for i in range(3)]
    for i, g in enumerate(rest):
        others = sum(lax.rem(h, 3) for h in rest if h is not g)
        at = jnp.where(g == 0, 3 - others, lax.rem(g, 3))
        for e in range(2):
            piece(PERIOD * FIXED + 2 * at + e, 2 * (PERIOD + i) + e, *orphan)
    index = sam[...]
    wide[pl.ds(SLOTS, 128, stride=ROWS), :] = (index >> 4).astype(F32).T
    wide[pl.ds(SLOTS + 1, 128, stride=ROWS), :] = (index & 15).astype(F32).T

    parts = sent.shape[0]
    span = 128 // parts
    copies = []
    for n in range(parts):

        def narrow(q, _):
            q = span // 4 * n + q
            ready[pl.ds(4 * q, 4)] = wide[pl.ds(4 * q * ROWS, 4 * ROWS), :].reshape(4, ROWS, 128).astype(BF)
            return 0

        lax.fori_loop(0, span // 4, narrow, 0, unroll=2)
        at = pl.ds(span * n, span)
        copies.append(pltpu.make_async_copy(ready.at[at], out.at[at], sent.at[n]))
        copies[-1].start()
    for copy in copies:
        copy.wait()


def pool(*arrays):
    return pl.pallas_call(
        pool_kernel,
        out_shape=jax.ShapeDtypeStruct((128, ROWS, 128), BF),
        in_specs=[pl.BlockSpec(memory_space=pl.ANY)] * 8,
        out_specs=pl.BlockSpec(memory_space=pl.ANY),
        scratch_shapes=[
            pltpu.VMEM((128 * ROWS, 128), F32),
            pltpu.VMEM((128, 128), jnp.int32),
            pltpu.VMEM((128, ROWS, 128), BF),
        ]
        + [pltpu.VMEM(a.shape, a.dtype) for a in arrays]
        + [pltpu.SemaphoreType.DMA((12,)), pltpu.SemaphoreType.DMA((4,))],
        compiler_params=pltpu.CompilerParams(vmem_limit_bytes=60 << 20),
        cost_estimate=pl.CostEstimate(flops=84 * 128 * 128 * 256, transcendentals=0, bytes_accessed=6 << 20),
    )(*arrays)


def tail_kernel(
    label, given, bottom, given_weights, bias, last, last_bias, marks, logits, loss,
    wide, hi, lo, stack, turned, packed, recv, weights, came, sem,
):
    parts = came.shape[0]
    span = 128 // parts
    copies = []
    for n in range(parts):
        at = pl.ds(span * n, span)
        copies.append(pltpu.make_async_copy(given.at[at], recv.at[at], came.at[n]))
        copies[-1].start()
    fetch = pltpu.make_async_copy(given_weights, weights, sem)
    fetch.start()
    zero = jnp.zeros((), BF)
    ones = lax.broadcasted_iota(jnp.int32, (16, 128), 0).astype(F32).astype(BF)

    def widen(p, _):
        wide[pl.ds(4 * p * ROWS, 4 * ROWS), :] = recv[pl.ds(4 * p, 4)].astype(F32).reshape(4 * ROWS, 128)
        return 0

    for n in range(parts):
        copies[n].wait()
        lax.fori_loop(span // 4 * n, span // 4 * (n + 1), widen, 0, unroll=2)
    hi[...] = wide[pl.ds(SLOTS, 128, stride=ROWS), :].T
    lo[...] = wide[pl.ds(SLOTS + 1, 128, stride=ROWS), :].T

    def put(f, value):
        stack[f] = value
        for k in range(8):
            turned[pl.ds(f * BATCH + k, BATCH // 8, stride=8), :] = stack[f, pl.ds(7 - k, BATCH // 8, stride=8), :]

    put(0, bottom[...].astype(BF).astype(F32))
    turned[(F + 1) * BATCH :, :] = jnp.zeros(((31 - F) * BATCH, 128), F32)

    def hits(slot, keep=None):
        high = hi[pl.ds(slot, 1), :]
        if keep is not None:
            high = jnp.where(keep, high, 63.0)
        high = jnp.broadcast_to(high, (16, 128)).astype(BF)
        low = jnp.broadcast_to(lo[pl.ds(slot, 1), :], (16, 128)).astype(BF)
        low = jnp.where(low == ones, jnp.ones((), BF), zero)
        return jnp.concatenate([jnp.where(high == jnp.asarray(h, BF), low, zero) for h in range(32)], axis=0)

    def rows(slot):
        return wide[pl.ds(slot, 128, stride=ROWS), :].astype(BF)

    def pooled(g, places):
        for e in range(2):
            slots = [(FIXED * g + 2 * n + e, None) for n in range(3)]
            for at in places:
                keep = label[pl.ds(at, 1), :] == jnp.asarray(g, jnp.int32)
                slots.append((PERIOD * FIXED + 2 * at + e, keep))
            left = jnp.concatenate([hits(s, keep) for s, keep in slots], axis=1)
            right = jnp.concatenate([rows(s) for s, _ in slots], axis=0)
            total = jnp.dot(left, right, preferred_element_type=F32)
            put(1 + 2 * g + e, total.astype(BF).astype(F32))

    pooled(0, [0, 1, 2])

    def group(g, _):
        pooled(g, [lax.rem(g, 3)])
        return 0

    lax.fori_loop(1, PERIOD, group, 0, unroll=4)

    packed[:, :128] = bottom[...].astype(BF)
    own = lax.broadcasted_iota(jnp.int32, (8, 128), 1) % 8 == 7 - lax.broadcasted_iota(jnp.int32, (8, 128), 0)

    def interact(m, _):
        halves = []
        for half in range(2):
            left = stack[:, pl.ds(16 * m + 8 * half, 8), :].reshape(8 * (F + 1), 128).astype(BF)
            right = [turned[pl.ds(j * BATCH + 16 * m + 8 * half, 8), :] for j in range(32)]
            right = jnp.concatenate(right, axis=0).astype(BF)
            gram = lax.dot_general(left, right, (((1,), (1,)), ((), ())), preferred_element_type=F32)
            columns = []
            for a in range(4):
                for tile in range(1 if a < 2 else 2):
                    total = None
                    for c in range(8):
                        i = 8 * a + c
                        if i > F or 16 * tile >= i:
                            continue
                        part = jnp.where(own, gram[8 * i : 8 * i + 8, 128 * tile : 128 * tile + 128], 0.0)
                        part = pltpu.roll(part, c, 1, stride=1, stride_axis=0)
                        total = part if total is None else total + part
                    columns.append(total)
            halves.append(jnp.concatenate(columns, axis=1))
        packed[pl.ds(pl.multiple_of(16 * m, 16), 16), 128:] = jnp.concatenate(halves, axis=0).astype(BF)
        return 0

    lax.fori_loop(0, BATCH // 16, interact, 0, unroll=4)

    fetch.wait()
    for m in range(4):
        at = pl.ds(128 * m, 128)
        hidden = jnp.dot(packed[at, :], weights[...], preferred_element_type=F32)
        hidden = jnp.maximum(hidden + bias[...], 0.0).astype(BF)
        out = lax.dot_general(last[...], hidden, (((1,), (1,)), ((), ())), preferred_element_type=F32)
        logits[:, at] = out[:1] + last_bias[0]
    x = logits[...]
    soft = jnp.maximum(x, 0.0) + jnp.log1p(jnp.exp(-jnp.abs(x)))
    term = jnp.sum(soft - marks[...].astype(F32) * x)
    loss[...] = jnp.full(loss.shape, term, F32)


def tail(label, recv, bottom, weights, bias, last, last_bias, marks):
    return pl.pallas_call(
        tail_kernel,
        out_shape=(jax.ShapeDtypeStruct((1, BATCH), F32), jax.ShapeDtypeStruct((1, 128), F32)),
        in_specs=[VMEM, pl.BlockSpec(memory_space=pl.ANY)] * 2 + [VMEM, VMEM, SMEM, VMEM],
        out_specs=(VMEM, VMEM),
        scratch_shapes=[
            pltpu.VMEM((128 * ROWS, 128), F32),
            pltpu.VMEM((128, 128), F32),
            pltpu.VMEM((128, 128), F32),
            pltpu.VMEM((F + 1, BATCH, 128), F32),
            pltpu.VMEM((32 * BATCH, 128), F32),
            pltpu.VMEM((BATCH, QW), BF),
            pltpu.VMEM((128, ROWS, 128), BF),
            pltpu.VMEM((QW, 1024), BF),
            pltpu.SemaphoreType.DMA((4,)),
            pltpu.SemaphoreType.DMA,
        ],
        compiler_params=pltpu.CompilerParams(vmem_limit_bytes=60 << 20),
        cost_estimate=pl.CostEstimate(flops=6 << 30, transcendentals=0, bytes_accessed=5 << 20),
    )(label, recv, bottom, weights, bias, last, last_bias, marks)


def labels_by_holder():
    label = np.full((8, 128), -1, np.int32)
    label[:3] = LABEL[np.arange(128) % PERIOD].T
    return label


def exchange(value, axes):
    return lax.all_to_all(value, axes, split_axis=0, concat_axis=0, tiled=True)


def ring_sum(value, axis, size, step):
    for other in ((1, 0, 3, 2), (3, 2, 1, 0)):
        pairs = [(i, i + (other[i // step % 4] - i // step % 4) * step) for i in range(size)]
        value = value + lax.ppermute(value, axis, pairs)
    return value


def keep_kernel(given, out):
    out[...] = given[...]


def keep(value):
    block = pl.BlockSpec((8,) + value.shape[1:], lambda n: (n, 0, 0))
    return pl.pallas_call(
        keep_kernel,
        grid=(value.shape[0] // 8,),
        out_shape=jax.ShapeDtypeStruct(value.shape, value.dtype),
        in_specs=[block],
        out_specs=block,
        compiler_params=pltpu.CompilerParams(vmem_limit_bytes=60 << 20),
        cost_estimate=pl.CostEstimate(flops=0, transcendentals=0, bytes_accessed=4 << 20),
    )(value)


def per_device(
    resident_row_blocks,
    orphan_blocks,
    home_offsets,
    home_lengths,
    home_samples,
    orphan_offsets,
    orphan_lengths,
    orphan_samples,
    orphan_owner,
    dense_inputs,
    labels,
    bottom_first,
    bias_first,
    bottom_second,
    bias_second,
    bottom_third,
    bias_third,
    top_hidden,
    bias_hidden,
    top_logit,
    bias_logit,
):
    chips = lax.axis_size("chip")
    outgoing = route(orphan_owner[:, 0], orphan_blocks, chips)
    pieces = pool(
        resident_row_blocks,
        orphan_blocks,
        home_offsets.transpose(0, 2, 1),
        home_lengths,
        home_samples,
        orphan_offsets.transpose(0, 2, 1),
        orphan_lengths,
        orphan_samples,
    )
    arrived = exchange(pieces, ALL)
    first = jax.nn.relu(
        jnp.dot(dense_inputs, bottom_first, preferred_element_type=F32) + bias_first
    ).astype(BF)
    second = jax.nn.relu(
        jnp.dot(first, bottom_second, preferred_element_type=F32) + bias_second
    ).astype(BF)
    bottom = jax.nn.relu(jnp.dot(second, bottom_third, preferred_element_type=F32) + bias_third)
    padded = jnp.concatenate([top_hidden, jnp.zeros((1, top_hidden.shape[1]), BF)], axis=0)
    weights = jnp.take(padded, jnp.asarray(FEATURE_ROWS), axis=0)
    last = jnp.broadcast_to(top_logit.reshape(1, -1), (8, top_logit.shape[0]))
    outgoing, weights, bottom, last = lax.optimization_barrier((outgoing, weights, bottom, last))
    rehomed = exchange(outgoing, "chip")
    logits, term = tail(
        jnp.asarray(labels_by_holder()),
        arrived,
        bottom,
        weights,
        bias_hidden[None, :],
        last,
        bias_logit,
        labels[None, :],
    )
    term = ring_sum(term, "hst", lax.axis_size("hst"), 1)
    term = term + lax.ppermute(term, "chip", [(i, i ^ 1) for i in range(chips)])
    term = ring_sum(term, "chip", chips, 2)
    rehomed, term = lax.optimization_barrier((keep(rehomed), term))
    term = ring_sum(term, "chip", chips, 8)
    return rehomed, logits[0], term[0, 0]


def solution(mesh):
    split = P(ALL)
    return jax.shard_map(
        per_device,
        mesh=mesh,
        in_specs=(split,) * 11 + (P(),) * 10,
        out_specs=(split, split, P()),
        check_vma=False,
    )
```

```python
import functools

import jax
import jax.numpy as jnp
import numpy as np
from jax import lax
from jax.experimental import pallas as pl
from jax.experimental.pallas import tpu as pltpu
from jax.sharding import PartitionSpec as P

ALL = ("hst", "chip")
PERIOD = 13
HOME, ORPHAN = 48, 32
FIXED = 6
SLOTS = 84
ROWS = 88
F = 26
BATCH = 512
NONE = 1023
QW = 896
BF, F32 = jnp.bfloat16, jnp.float32
VMEM = pl.BlockSpec(memory_space=pltpu.VMEM)
SMEM = pl.BlockSpec(memory_space=pltpu.SMEM)


def slot_tables():
    table = np.full((PERIOD, 128), -1, np.int32)
    label = np.full((PERIOD, 3), -1, np.int32)
    for r in range(PERIOD):
        for g in range(PERIOD):
            k = (g - 11 * r) % PERIOD
            o = (g - 4 - 3 * r) % PERIOD
            for e in range(2):
                table[r, FIXED * g + e] = 2 * k + e
                if k + PERIOD < HOME // 2:
                    table[r, FIXED * g + 2 + e] = 2 * (k + PERIOD) + e
                table[r, FIXED * g + 4 + e] = 2 * o + e
        rest = [(PERIOD + i, (4 + 3 * r + i) % PERIOD) for i in range(3)]
        free = [0, 1, 2]
        for k, g in sorted(rest, key=lambda item: item[1] == 0):
            at = g % 3 if g % 3 in free else free[0]
            free.remove(at)
            label[r, at] = g
            for e in range(2):
                table[r, PERIOD * FIXED + 2 * at + e] = 2 * k + e
    for g in range(1, PERIOD):
        assert all(at == g % 3 for r in range(PERIOD) for at in range(3) if label[r, at] == g)
    return table, label


def feature_rows():
    rows = np.full((QW,), 479, np.int32)
    rows[:128] = np.arange(128)
    at = 128
    for a in range(4):
        for tile in range(1 if a < 2 else 2):
            for lane in range(128):
                turn = (lane - 7) % 128
                i, j = 8 * a + turn % 8, 16 * tile + turn // 8
                if j < i <= F:
                    rows[at + lane] = 128 + i * (i - 1) // 2 + j
            at += 128
    return rows


TABLE, LABEL = slot_tables()
FEATURE_ROWS = feature_rows()


def route_kernel(owner, orphans, out, count):
    slots = out.shape[0] // count.shape[0]

    def clear(c, _):
        count[c] = 0
        return 0

    lax.fori_loop(0, count.shape[0], clear, 0)
    out[...] = jnp.zeros_like(out)

    def place(i, _):
        o = owner[i]
        n = count[o]
        out[slots * o + n] = orphans[i]
        count[o] = n + 1
        return 0

    lax.fori_loop(0, orphans.shape[0], place, 0)


def route(orphan_owner, orphans, chips):
    return pl.pallas_call(
        route_kernel,
        out_shape=jax.ShapeDtypeStruct((2 * chips,) + orphans.shape[1:], BF),
        in_specs=[SMEM, VMEM],
        out_specs=VMEM,
        scratch_shapes=[pltpu.SMEM((chips,), jnp.int32)],
        compiler_params=pltpu.CompilerParams(vmem_limit_bytes=16 << 20),
        cost_estimate=pl.CostEstimate(flops=0, transcendentals=0, bytes_accessed=3 << 20),
    )(orphan_owner, orphans)


def pool_kernel(*refs):
    given, out, (wide, sam, ready), held, sem, sent = refs[:8], refs[8], refs[9:12], refs[12:20], refs[20], refs[21]
    cuts = [(n, None) for n in range(2, 8)] + [(0, (0, 12)), (0, (26, 38)), (1, (0, 12))]
    cuts = [cuts, [(0, (12, 26)), (0, (38, 48)), (1, (12, 32))]]
    waves = []
    for wave in cuts:
        copies = []
        for n, cut in wave:
            at = pl.ds(cut[0], cut[1] - cut[0]) if cut else pl.ds(0, given[n].shape[0])
            number = len(copies) + 9 * len(waves)
            copies.append(pltpu.make_async_copy(given[n].at[at], held[n].at[at], sem.at[number]))
            copies[-1].start()
        waves.append(copies)
    home, orphan = (held[0],) + tuple(held[2:5]), (held[1],) + tuple(held[5:8])
    me = lax.axis_index("hst") * lax.axis_size("chip") + lax.axis_index("chip")
    rows = lax.broadcasted_iota(jnp.int32, (128, 128), 0).astype(F32).astype(BF)
    place = lax.broadcasted_iota(jnp.int32, (8, 128), 0)
    one, zero = jnp.ones((), BF), jnp.zeros((), BF)
    sam[...] = jnp.full(sam.shape, NONE, jnp.int32)
    for s in range(SLOTS + 2, ROWS):
        wide[pl.ds(s, 128, stride=ROWS), :] = jnp.zeros((128, 128), F32)
    for copy in waves[0]:
        copy.wait()

    def piece(slot, b, blocks, off, length, samples):
        live = jnp.where(place < length[pl.ds(b, 1), :], off[b], -1).astype(F32).astype(BF)
        counts = jnp.zeros((128, 128), BF)
        for n in range(8):
            counts = counts + jnp.where(rows == live[n : n + 1, :], one, zero)
        sums = lax.dot_general(counts, blocks[b], (((0,), (0,)), ((), ())), preferred_element_type=F32)
        wide[pl.ds(slot, 128, stride=ROWS), :] = sums
        sam[pl.ds(slot, 1), :] = samples[pl.ds(b, 1), :]

    def pair(k, more):
        g = FIXED * lax.rem(11 * me + k, PERIOD)
        for e in range(2):
            piece(g + e, 2 * k + e, *home)
        for e in range(2):
            if more:
                piece(g + 2 + e, 2 * (k + PERIOD) + e, *home)
            else:
                wide[pl.ds(g + 2 + e, 128, stride=ROWS), :] = jnp.zeros((128, 128), F32)
        g = FIXED * lax.rem(4 + 3 * me + k, PERIOD)
        for e in range(2):
            piece(g + 4 + e, 2 * k + e, *orphan)

    def step(k, _):
        pair(k, True)
        return 0

    both = HOME // 2 - PERIOD
    lax.fori_loop(0, 6, step, 0, unroll=3)
    for copy in waves[1]:
        copy.wait()
    lax.fori_loop(6, both, step, 0, unroll=5)
    for k in range(both, PERIOD):
        pair(k, False)
    rest = [lax.rem(4 + 3 * me + i, PERIOD) for i in range(3)]
    for i, g in enumerate(rest):
        others = sum(lax.rem(h, 3) for h in rest if h is not g)
        at = jnp.where(g == 0, 3 - others, lax.rem(g, 3))
        for e in range(2):
            piece(PERIOD * FIXED + 2 * at + e, 2 * (PERIOD + i) + e, *orphan)
    index = sam[...]
    wide[pl.ds(SLOTS, 128, stride=ROWS), :] = (index >> 4).astype(F32).T
    wide[pl.ds(SLOTS + 1, 128, stride=ROWS), :] = (index & 15).astype(F32).T

    parts = sent.shape[0]
    span = 128 // parts
    copies = []
    for n in range(parts):

        def narrow(q, _):
            q = span // 4 * n + q
            ready[pl.ds(4 * q, 4)] = wide[pl.ds(4 * q * ROWS, 4 * ROWS), :].reshape(4, ROWS, 128).astype(BF)
            return 0

        lax.fori_loop(0, span // 4, narrow, 0, unroll=2)
        at = pl.ds(span * n, span)
        copies.append(pltpu.make_async_copy(ready.at[at], out.at[at], sent.at[n]))
        copies[-1].start()
    for copy in copies:
        copy.wait()


def pool(*arrays):
    return pl.pallas_call(
        pool_kernel,
        out_shape=jax.ShapeDtypeStruct((128, ROWS, 128), BF),
        in_specs=[pl.BlockSpec(memory_space=pl.ANY)] * 8,
        out_specs=pl.BlockSpec(memory_space=pl.ANY),
        scratch_shapes=[
            pltpu.VMEM((128 * ROWS, 128), F32),
            pltpu.VMEM((128, 128), jnp.int32),
            pltpu.VMEM((128, ROWS, 128), BF),
        ]
        + [pltpu.VMEM(a.shape, a.dtype) for a in arrays]
        + [pltpu.SemaphoreType.DMA((12,)), pltpu.SemaphoreType.DMA((4,))],
        compiler_params=pltpu.CompilerParams(vmem_limit_bytes=60 << 20),
        cost_estimate=pl.CostEstimate(flops=84 * 128 * 128 * 256, transcendentals=0, bytes_accessed=6 << 20),
    )(*arrays)


def tail_kernel(
    label, given, bottom, given_weights, bias, last, last_bias, marks, logits, loss,
    wide, hi, lo, stack, packed, recv, weights, came, sem,
):
    parts = came.shape[0]
    span = 128 // parts
    copies = []
    for n in range(parts):
        at = pl.ds(span * n, span)
        copies.append(pltpu.make_async_copy(given.at[at], recv.at[at], came.at[n]))
        copies[-1].start()
    fetch = pltpu.make_async_copy(given_weights, weights, sem)
    fetch.start()
    zero = jnp.zeros((), BF)
    ones = lax.broadcasted_iota(jnp.int32, (16, 128), 0).astype(F32).astype(BF)

    def widen(p, _):
        wide[pl.ds(4 * p * ROWS, 4 * ROWS), :] = recv[pl.ds(4 * p, 4)].astype(F32).reshape(4 * ROWS, 128)
        return 0

    for n in range(parts):
        copies[n].wait()
        lax.fori_loop(span // 4 * n, span // 4 * (n + 1), widen, 0, unroll=2)
    hi[...] = wide[pl.ds(SLOTS, 128, stride=ROWS), :].T
    lo[...] = wide[pl.ds(SLOTS + 1, 128, stride=ROWS), :].T

    stack[0] = bottom[...].astype(BF).astype(F32)

    def hits(slot, keep=None):
        high = hi[pl.ds(slot, 1), :]
        if keep is not None:
            high = jnp.where(keep, high, 63.0)
        high = jnp.broadcast_to(high, (16, 128)).astype(BF)
        low = jnp.broadcast_to(lo[pl.ds(slot, 1), :], (16, 128)).astype(BF)
        low = jnp.where(low == ones, jnp.ones((), BF), zero)
        return jnp.concatenate([jnp.where(high == jnp.asarray(h, BF), low, zero) for h in range(32)], axis=0)

    def rows(slot):
        return wide[pl.ds(slot, 128, stride=ROWS), :].astype(BF)

    def pooled(g, places):
        for e in range(2):
            slots = [(FIXED * g + 2 * n + e, None) for n in range(3)]
            for at in places:
                keep = label[pl.ds(at, 1), :] == jnp.asarray(g, jnp.int32)
                slots.append((PERIOD * FIXED + 2 * at + e, keep))
            left = jnp.concatenate([hits(s, keep) for s, keep in slots], axis=1)
            right = jnp.concatenate([rows(s) for s, _ in slots], axis=0)
            total = jnp.dot(left, right, preferred_element_type=F32)
            stack[1 + 2 * g + e] = total.astype(BF).astype(F32)

    pooled(0, [0, 1, 2])

    def group(g, _):
        pooled(g, [lax.rem(g, 3)])
        return 0

    lax.fori_loop(1, PERIOD, group, 0, unroll=4)

    packed[:, :128] = bottom[...].astype(BF)
    own = lax.broadcasted_iota(jnp.int32, (8, 128), 1) % 8 == 7 - lax.broadcasted_iota(jnp.int32, (8, 128), 0)

    back = 7 - lax.broadcasted_iota(jnp.int32, (8, 128), 0)

    def interact(m, _):
        halves = []
        for half in range(2):
            left = stack[:, pl.ds(16 * m + 8 * half, 8), :].reshape(8 * (F + 1), 128).astype(BF)
            right = [jnp.take_along_axis(stack[j, pl.ds(16 * m + 8 * half, 8), :], back, axis=0) for j in range(F + 1)]
            right = jnp.concatenate(right + [jnp.zeros((8 * (31 - F), 128), F32)], axis=0).astype(BF)
            gram = lax.dot_general(left, right, (((1,), (1,)), ((), ())), preferred_element_type=F32)
            columns = []
            for a in range(4):
                for tile in range(1 if a < 2 else 2):
                    total = None
                    for c in range(8):
                        i = 8 * a + c
                        if i > F or 16 * tile >= i:
                            continue
                        part = jnp.where(own, gram[8 * i : 8 * i + 8, 128 * tile : 128 * tile + 128], 0.0)
                        part = pltpu.roll(part, c, 1, stride=1, stride_axis=0)
                        total = part if total is None else total + part
                    columns.append(total)
            halves.append(jnp.concatenate(columns, axis=1))
        packed[pl.ds(pl.multiple_of(16 * m, 16), 16), 128:] = jnp.concatenate(halves, axis=0).astype(BF)
        return 0

    lax.fori_loop(0, BATCH // 16, interact, 0, unroll=8)

    fetch.wait()
    hidden = jnp.dot(packed[...], weights[...], preferred_element_type=F32)
    hidden = jnp.maximum(hidden + bias[...], 0.0).astype(BF)
    out = lax.dot_general(last[...], hidden, (((1,), (1,)), ((), ())), preferred_element_type=F32)
    x = out[:1] + last_bias[0]
    logits[...] = x
    soft = jnp.maximum(x, 0.0) + jnp.log1p(jnp.exp(-jnp.abs(x)))
    term = jnp.sum(soft - marks[...].astype(F32) * x)
    loss[...] = jnp.full(loss.shape, term, F32)


def tail(label, recv, bottom, weights, bias, last, last_bias, marks):
    return pl.pallas_call(
        tail_kernel,
        out_shape=(jax.ShapeDtypeStruct((1, BATCH), F32), jax.ShapeDtypeStruct((1, 128), F32)),
        in_specs=[VMEM, pl.BlockSpec(memory_space=pl.ANY)] * 2 + [VMEM, VMEM, SMEM, VMEM],
        out_specs=(VMEM, VMEM),
        scratch_shapes=[
            pltpu.VMEM((128 * ROWS, 128), F32),
            pltpu.VMEM((128, 128), F32),
            pltpu.VMEM((128, 128), F32),
            pltpu.VMEM((F + 1, BATCH, 128), F32),
            pltpu.VMEM((BATCH, QW), BF),
            pltpu.VMEM((128, ROWS, 128), BF),
            pltpu.VMEM((QW, 1024), BF),
            pltpu.SemaphoreType.DMA((4,)),
            pltpu.SemaphoreType.DMA,
        ],
        compiler_params=pltpu.CompilerParams(vmem_limit_bytes=36 << 20),
        cost_estimate=pl.CostEstimate(flops=6 << 30, transcendentals=0, bytes_accessed=5 << 20),
    )(label, recv, bottom, weights, bias, last, last_bias, marks)


def labels_by_holder():
    label = np.full((8, 128), -1, np.int32)
    label[:3] = LABEL[np.arange(128) % PERIOD].T
    return label


def exchange(value, axes):
    return lax.all_to_all(value, axes, split_axis=0, concat_axis=0, tiled=True)


def near_sum(value, axis, size, step):
    for other in ((1, 0, 3, 2), (3, 2, 1, 0)):
        pairs = [(i, i + (other[i // step % 4] - i // step % 4) * step) for i in range(size)]
        value = value + lax.ppermute(value, axis, pairs)
    return value


def ring_sum(value, axis):
    one, two, three = (lax.ppermute(value, axis, [(i, (i + k) % 4) for i in range(4)]) for k in (1, 2, 3))
    return (value + two) + (one + three)


def keep_kernel(given, out, sent):
    span = given.shape[0] // sent.shape[0]
    copies = []
    for n in range(sent.shape[0]):
        at = pl.ds(span * n, span)
        copies.append(pltpu.make_async_copy(given.at[at], out.at[at], sent.at[n]))
        copies[-1].start()
    for copy in copies:
        copy.wait()


def keep(value):
    return pl.pallas_call(
        keep_kernel,
        out_shape=jax.ShapeDtypeStruct(value.shape, value.dtype),
        in_specs=[VMEM],
        out_specs=pl.BlockSpec(memory_space=pl.ANY),
        scratch_shapes=[pltpu.SemaphoreType.DMA((8,))],
        compiler_params=pltpu.CompilerParams(vmem_limit_bytes=8 << 20),
        cost_estimate=pl.CostEstimate(flops=0, transcendentals=0, bytes_accessed=4 << 20),
    )(value)


def per_device(
    resident_row_blocks,
    orphan_blocks,
    home_offsets,
    home_lengths,
    home_samples,
    orphan_offsets,
    orphan_lengths,
    orphan_samples,
    orphan_owner,
    dense_inputs,
    labels,
    bottom_first,
    bias_first,
    bottom_second,
    bias_second,
    bottom_third,
    bias_third,
    top_hidden,
    bias_hidden,
    top_logit,
    bias_logit,
):
    chips = lax.axis_size("chip")
    outgoing = route(orphan_owner[:, 0], orphan_blocks, chips)
    pieces = pool(
        resident_row_blocks,
        orphan_blocks,
        home_offsets.transpose(0, 2, 1),
        home_lengths,
        home_samples,
        orphan_offsets.transpose(0, 2, 1),
        orphan_lengths,
        orphan_samples,
    )
    arrived = exchange(pieces, ALL)
    first = jax.nn.relu(
        jnp.dot(dense_inputs, bottom_first, preferred_element_type=F32) + bias_first
    ).astype(BF)
    second = jax.nn.relu(
        jnp.dot(first, bottom_second, preferred_element_type=F32) + bias_second
    ).astype(BF)
    bottom = jax.nn.relu(jnp.dot(second, bottom_third, preferred_element_type=F32) + bias_third)
    padded = jnp.concatenate([top_hidden, jnp.zeros((1, top_hidden.shape[1]), BF)], axis=0)
    weights = jnp.take(padded, jnp.asarray(FEATURE_ROWS), axis=0)
    last = jnp.broadcast_to(top_logit.reshape(1, -1), (8, top_logit.shape[0]))
    outgoing, weights, bottom, last = lax.optimization_barrier((outgoing, weights, bottom, last))
    rehomed = exchange(outgoing, "chip")
    logits, term = tail(
        jnp.asarray(labels_by_holder()),
        arrived,
        bottom,
        weights,
        bias_hidden[None, :],
        last,
        bias_logit,
        labels[None, :],
    )
    term = ring_sum(term, "hst")
    term = term + lax.ppermute(term, "chip", [(i, i ^ 1) for i in range(chips)])
    term = near_sum(term, "chip", chips, 2)
    rehomed, term = lax.optimization_barrier((keep(rehomed), term))
    term = near_sum(term, "chip", chips, 8)
    return rehomed, logits[0], term[0, 0]


def solution(mesh):
    split = P(ALL)
    return jax.shard_map(
        per_device,
        mesh=mesh,
        in_specs=(split,) * 11 + (P(),) * 10,
        out_specs=(split, split, P()),
        check_vma=False,
    )
```

```python
import functools

import jax
import jax.numpy as jnp
import numpy as np
from jax import lax
from jax.experimental import pallas as pl
from jax.experimental.pallas import tpu as pltpu
from jax.sharding import PartitionSpec as P

ALL = ("hst", "chip")
PERIOD = 13
HOME, ORPHAN = 48, 32
FIXED = 6
SLOTS = 84
ROWS = 88
F = 26
BATCH = 512
NONE = 1023
QW = 896
BF, F32 = jnp.bfloat16, jnp.float32
VMEM = pl.BlockSpec(memory_space=pltpu.VMEM)
SMEM = pl.BlockSpec(memory_space=pltpu.SMEM)


def slot_tables():
    table = np.full((PERIOD, 128), -1, np.int32)
    label = np.full((PERIOD, 3), -1, np.int32)
    for r in range(PERIOD):
        for g in range(PERIOD):
            k = (g - 11 * r) % PERIOD
            o = (g - 4 - 3 * r) % PERIOD
            for e in range(2):
                table[r, FIXED * g + e] = 2 * k + e
                if k + PERIOD < HOME // 2:
                    table[r, FIXED * g + 2 + e] = 2 * (k + PERIOD) + e
                table[r, FIXED * g + 4 + e] = 2 * o + e
        rest = [(PERIOD + i, (4 + 3 * r + i) % PERIOD) for i in range(3)]
        free = [0, 1, 2]
        for k, g in sorted(rest, key=lambda item: item[1] == 0):
            at = g % 3 if g % 3 in free else free[0]
            free.remove(at)
            label[r, at] = g
            for e in range(2):
                table[r, PERIOD * FIXED + 2 * at + e] = 2 * k + e
    for g in range(1, PERIOD):
        assert all(at == g % 3 for r in range(PERIOD) for at in range(3) if label[r, at] == g)
    return table, label


def feature_rows():
    rows = np.full((QW,), 479, np.int32)
    rows[:128] = np.arange(128)
    at = 128
    for a in range(4):
        for tile in range(1 if a < 2 else 2):
            for lane in range(128):
                turn = (lane - 7) % 128
                i, j = 8 * a + turn % 8, 16 * tile + turn // 8
                if j < i <= F:
                    rows[at + lane] = 128 + i * (i - 1) // 2 + j
            at += 128
    return rows


TABLE, LABEL = slot_tables()
FEATURE_ROWS = feature_rows()


def route_kernel(owner, orphans, out, count):
    slots = out.shape[0] // count.shape[0]

    def clear(c, _):
        count[c] = 0
        return 0

    lax.fori_loop(0, count.shape[0], clear, 0)
    out[...] = jnp.zeros_like(out)

    def place(i, _):
        o = owner[i]
        n = count[o]
        out[slots * o + n] = orphans[i]
        count[o] = n + 1
        return 0

    lax.fori_loop(0, orphans.shape[0], place, 0)


def route(orphan_owner, orphans, chips):
    return pl.pallas_call(
        route_kernel,
        out_shape=jax.ShapeDtypeStruct((2 * chips,) + orphans.shape[1:], BF),
        in_specs=[SMEM, VMEM],
        out_specs=VMEM,
        scratch_shapes=[pltpu.SMEM((chips,), jnp.int32)],
        compiler_params=pltpu.CompilerParams(vmem_limit_bytes=16 << 20),
        cost_estimate=pl.CostEstimate(flops=0, transcendentals=0, bytes_accessed=3 << 20),
    )(orphan_owner, orphans)


def pool_kernel(*refs):
    given, out, (wide, sam, ready), held, sem, sent = refs[:8], refs[8], refs[9:12], refs[12:20], refs[20], refs[21]
    cuts = [(n, None) for n in range(2, 8)] + [(0, (0, 12)), (0, (26, 38)), (1, (0, 12))]
    cuts = [cuts, [(0, (12, 26)), (0, (38, 48)), (1, (12, 32))]]
    waves = []
    for wave in cuts:
        copies = []
        for n, cut in wave:
            at = pl.ds(cut[0], cut[1] - cut[0]) if cut else pl.ds(0, given[n].shape[0])
            number = len(copies) + 9 * len(waves)
            copies.append(pltpu.make_async_copy(given[n].at[at], held[n].at[at], sem.at[number]))
            copies[-1].start()
        waves.append(copies)
    home, orphan = (held[0],) + tuple(held[2:5]), (held[1],) + tuple(held[5:8])
    me = lax.axis_index("hst") * lax.axis_size("chip") + lax.axis_index("chip")
    rows = lax.broadcasted_iota(jnp.int32, (128, 128), 0).astype(F32).astype(BF)
    place = lax.broadcasted_iota(jnp.int32, (8, 128), 0)
    one, zero = jnp.ones((), BF), jnp.zeros((), BF)
    sam[...] = jnp.full(sam.shape, NONE, jnp.int32)
    for s in range(SLOTS + 2, ROWS):
        wide[pl.ds(s, 128, stride=ROWS), :] = jnp.zeros((128, 128), F32)
    for copy in waves[0]:
        copy.wait()

    def piece(slot, b, blocks, off, length, samples):
        live = jnp.where(place < length[pl.ds(b, 1), :], off[b], -1).astype(F32).astype(BF)
        counts = jnp.zeros((128, 128), BF)
        for n in range(8):
            counts = counts + jnp.where(rows == live[n : n + 1, :], one, zero)
        sums = lax.dot_general(counts, blocks[b], (((0,), (0,)), ((), ())), preferred_element_type=F32)
        wide[pl.ds(slot, 128, stride=ROWS), :] = sums
        sam[pl.ds(slot, 1), :] = samples[pl.ds(b, 1), :]

    def pair(k, more):
        g = FIXED * lax.rem(11 * me + k, PERIOD)
        for e in range(2):
            piece(g + e, 2 * k + e, *home)
        for e in range(2):
            if more:
                piece(g + 2 + e, 2 * (k + PERIOD) + e, *home)
            else:
                wide[pl.ds(g + 2 + e, 128, stride=ROWS), :] = jnp.zeros((128, 128), F32)
        g = FIXED * lax.rem(4 + 3 * me + k, PERIOD)
        for e in range(2):
            piece(g + 4 + e, 2 * k + e, *orphan)

    def step(k, _):
        pair(k, True)
        return 0

    both = HOME // 2 - PERIOD
    lax.fori_loop(0, 6, step, 0, unroll=3)
    for copy in waves[1]:
        copy.wait()
    lax.fori_loop(6, both, step, 0, unroll=5)
    for k in range(both, PERIOD):
        pair(k, False)
    rest = [lax.rem(4 + 3 * me + i, PERIOD) for i in range(3)]
    for i, g in enumerate(rest):
        others = sum(lax.rem(h, 3) for h in rest if h is not g)
        at = jnp.where(g == 0, 3 - others, lax.rem(g, 3))
        for e in range(2):
            piece(PERIOD * FIXED + 2 * at + e, 2 * (PERIOD + i) + e, *orphan)
    index = sam[...]
    wide[pl.ds(SLOTS, 128, stride=ROWS), :] = (index >> 4).astype(F32).T
    wide[pl.ds(SLOTS + 1, 128, stride=ROWS), :] = (index & 15).astype(F32).T

    parts = sent.shape[0]
    span = 128 // parts
    copies = []
    for n in range(parts):

        def narrow(q, _):
            q = span // 4 * n + q
            ready[pl.ds(4 * q, 4)] = wide[pl.ds(4 * q * ROWS, 4 * ROWS), :].reshape(4, ROWS, 128).astype(BF)
            return 0

        lax.fori_loop(0, span // 4, narrow, 0, unroll=2)
        at = pl.ds(span * n, span)
        copies.append(pltpu.make_async_copy(ready.at[at], out.at[at], sent.at[n]))
        copies[-1].start()
    for copy in copies:
        copy.wait()


def pool(*arrays):
    return pl.pallas_call(
        pool_kernel,
        out_shape=jax.ShapeDtypeStruct((128, ROWS, 128), BF),
        in_specs=[pl.BlockSpec(memory_space=pl.ANY)] * 8,
        out_specs=pl.BlockSpec(memory_space=pl.ANY),
        scratch_shapes=[
            pltpu.VMEM((128 * ROWS, 128), F32),
            pltpu.VMEM((128, 128), jnp.int32),
            pltpu.VMEM((128, ROWS, 128), BF),
        ]
        + [pltpu.VMEM(a.shape, a.dtype) for a in arrays]
        + [pltpu.SemaphoreType.DMA((12,)), pltpu.SemaphoreType.DMA((4,))],
        compiler_params=pltpu.CompilerParams(vmem_limit_bytes=60 << 20),
        cost_estimate=pl.CostEstimate(flops=84 * 128 * 128 * 256, transcendentals=0, bytes_accessed=6 << 20),
    )(*arrays)


def tail_kernel(*refs):
    (given, *others), (logits, loss), refs = refs[:8], refs[8:10], refs[10:]
    recv, (label, bottom, weights, bias, last, last_bias, marks), refs = refs[0], refs[1:8], refs[8:]
    wide, hi, lo, stack, packed, came, sems = refs
    parts = came.shape[0]
    span = 128 // parts
    copies = []
    for n in range(parts):
        at = pl.ds(span * n, span)
        copies.append(pltpu.make_async_copy(given.at[at], recv.at[at], came.at[n]))
        copies[-1].start()
    held = (label, bottom, weights, bias, last, last_bias, marks)
    fetches = [pltpu.make_async_copy(g, h, sems.at[n]) for n, (g, h) in enumerate(zip(others, held))]
    for fetch in fetches:
        fetch.start()
    zero = jnp.zeros((), BF)
    ones = lax.broadcasted_iota(jnp.int32, (16, 128), 0).astype(F32).astype(BF)

    def widen(p, _):
        wide[pl.ds(4 * p * ROWS, 4 * ROWS), :] = recv[pl.ds(4 * p, 4)].astype(F32).reshape(4 * ROWS, 128)
        return 0

    for n in range(parts):
        copies[n].wait()
        lax.fori_loop(span // 4 * n, span // 4 * (n + 1), widen, 0, unroll=2)
    hi[...] = wide[pl.ds(SLOTS, 128, stride=ROWS), :].T
    lo[...] = wide[pl.ds(SLOTS + 1, 128, stride=ROWS), :].T

    for fetch in fetches[:2]:
        fetch.wait()
    stack[0] = bottom[...].astype(BF).astype(F32)

    def hits(slot, keep=None):
        high = hi[pl.ds(slot, 1), :]
        if keep is not None:
            high = jnp.where(keep, high, 63.0)
        high = jnp.broadcast_to(high, (16, 128)).astype(BF)
        low = jnp.broadcast_to(lo[pl.ds(slot, 1), :], (16, 128)).astype(BF)
        low = jnp.where(low == ones, jnp.ones((), BF), zero)
        return jnp.concatenate([jnp.where(high == jnp.asarray(h, BF), low, zero) for h in range(32)], axis=0)

    def rows(slot):
        return wide[pl.ds(slot, 128, stride=ROWS), :].astype(BF)

    def pooled(g, places):
        for e in range(2):
            slots = [(FIXED * g + 2 * n + e, None) for n in range(3)]
            for at in places:
                keep = label[pl.ds(at, 1), :] == jnp.asarray(g, jnp.int32)
                slots.append((PERIOD * FIXED + 2 * at + e, keep))
            left = jnp.concatenate([hits(s, keep) for s, keep in slots], axis=1)
            right = jnp.concatenate([rows(s) for s, _ in slots], axis=0)
            total = jnp.dot(left, right, preferred_element_type=F32)
            stack[1 + 2 * g + e] = total.astype(BF).astype(F32)

    pooled(0, [0, 1, 2])

    def group(g, _):
        pooled(g, [lax.rem(g, 3)])
        return 0

    lax.fori_loop(1, PERIOD, group, 0, unroll=4)

    packed[:, :128] = bottom[...].astype(BF)
    own = lax.broadcasted_iota(jnp.int32, (8, 128), 1) % 8 == 7 - lax.broadcasted_iota(jnp.int32, (8, 128), 0)

    back = 7 - lax.broadcasted_iota(jnp.int32, (8, 128), 0)

    def interact(m, _):
        halves = []
        for half in range(2):
            left = stack[:, pl.ds(16 * m + 8 * half, 8), :].reshape(8 * (F + 1), 128).astype(BF)
            right = [jnp.take_along_axis(stack[j, pl.ds(16 * m + 8 * half, 8), :], back, axis=0) for j in range(F + 1)]
            right = jnp.concatenate(right + [jnp.zeros((8 * (31 - F), 128), F32)], axis=0).astype(BF)
            gram = lax.dot_general(left, right, (((1,), (1,)), ((), ())), preferred_element_type=F32)
            columns = []
            for a in range(4):
                for tile in range(1 if a < 2 else 2):
                    total = None
                    for c in range(8):
                        i = 8 * a + c
                        if i > F or 16 * tile >= i:
                            continue
                        part = jnp.where(own, gram[8 * i : 8 * i + 8, 128 * tile : 128 * tile + 128], 0.0)
                        part = pltpu.roll(part, c, 1, stride=1, stride_axis=0)
                        total = part if total is None else total + part
                    columns.append(total)
            halves.append(jnp.concatenate(columns, axis=1))
        packed[pl.ds(pl.multiple_of(16 * m, 16), 16), 128:] = jnp.concatenate(halves, axis=0).astype(BF)
        return 0

    lax.fori_loop(0, BATCH // 16, interact, 0, unroll=8)

    for fetch in fetches[2:]:
        fetch.wait()
    hidden = jnp.dot(packed[...], weights[...], preferred_element_type=F32)
    hidden = jnp.maximum(hidden + bias[...], 0.0).astype(BF)
    out = lax.dot_general(last[...], hidden, (((1,), (1,)), ((), ())), preferred_element_type=F32)
    x = out[:1] + last_bias[:, :1]
    logits[...] = x
    soft = jnp.maximum(x, 0.0) + jnp.log1p(jnp.exp(-jnp.abs(x)))
    term = jnp.sum(soft - marks[...].astype(F32) * x)
    loss[...] = jnp.full(loss.shape, term, F32)


def tail(given, *others):
    anywhere = pl.BlockSpec(memory_space=pl.ANY)
    return pl.pallas_call(
        tail_kernel,
        out_shape=(jax.ShapeDtypeStruct((1, BATCH), F32), jax.ShapeDtypeStruct((1, 128), F32)),
        in_specs=[anywhere] * 8,
        out_specs=(VMEM, VMEM),
        scratch_shapes=[pltpu.VMEM(a.shape, a.dtype) for a in (given,) + others]
        + [
            pltpu.VMEM((128 * ROWS, 128), F32),
            pltpu.VMEM((128, 128), F32),
            pltpu.VMEM((128, 128), F32),
            pltpu.VMEM((F + 1, BATCH, 128), F32),
            pltpu.VMEM((BATCH, QW), BF),
            pltpu.SemaphoreType.DMA((4,)),
            pltpu.SemaphoreType.DMA((7,)),
        ],
        compiler_params=pltpu.CompilerParams(vmem_limit_bytes=60 << 20),
        cost_estimate=pl.CostEstimate(flops=6 << 30, transcendentals=0, bytes_accessed=5 << 20),
    )(given, *others)


def labels_by_holder():
    label = np.full((8, 128), -1, np.int32)
    label[:3] = LABEL[np.arange(128) % PERIOD].T
    return label


def exchange(value, axes):
    return lax.all_to_all(value, axes, split_axis=0, concat_axis=0, tiled=True)


def near_hop(value, axis, size, step, hop):
    other = ((1, 0, 3, 2), (3, 2, 1, 0))[hop]
    pairs = [(i, i + (other[i // step % 4] - i // step % 4) * step) for i in range(size)]
    return value + lax.ppermute(value, axis, pairs)


def ring_sum(value, axis):
    one, two, three = (lax.ppermute(value, axis, [(i, (i + k) % 4) for i in range(4)]) for k in (1, 2, 3))
    return (value + two) + (one + three)


def keep_kernel(given, out, sent):
    span = given.shape[0] // sent.shape[0]
    copies = []
    for n in range(sent.shape[0]):
        at = pl.ds(span * n, span)
        copies.append(pltpu.make_async_copy(given.at[at], out.at[at], sent.at[n]))
        copies[-1].start()
    for copy in copies:
        copy.wait()


def keep(value):
    return pl.pallas_call(
        keep_kernel,
        out_shape=jax.ShapeDtypeStruct(value.shape, value.dtype),
        in_specs=[VMEM],
        out_specs=pl.BlockSpec(memory_space=pl.ANY),
        scratch_shapes=[pltpu.SemaphoreType.DMA((8,))],
        compiler_params=pltpu.CompilerParams(vmem_limit_bytes=8 << 20),
        cost_estimate=pl.CostEstimate(flops=0, transcendentals=0, bytes_accessed=4 << 20),
    )(value)


def per_device(
    resident_row_blocks,
    orphan_blocks,
    home_offsets,
    home_lengths,
    home_samples,
    orphan_offsets,
    orphan_lengths,
    orphan_samples,
    orphan_owner,
    dense_inputs,
    labels,
    bottom_first,
    bias_first,
    bottom_second,
    bias_second,
    bottom_third,
    bias_third,
    top_hidden,
    bias_hidden,
    top_logit,
    bias_logit,
):
    chips = lax.axis_size("chip")
    outgoing = route(orphan_owner[:, 0], orphan_blocks, chips)
    pieces = pool(
        resident_row_blocks,
        orphan_blocks,
        home_offsets.transpose(0, 2, 1),
        home_lengths,
        home_samples,
        orphan_offsets.transpose(0, 2, 1),
        orphan_lengths,
        orphan_samples,
    )
    arrived = exchange(pieces, ALL)
    first = jax.nn.relu(
        jnp.dot(dense_inputs, bottom_first, preferred_element_type=F32) + bias_first
    ).astype(BF)
    second = jax.nn.relu(
        jnp.dot(first, bottom_second, preferred_element_type=F32) + bias_second
    ).astype(BF)
    bottom = jax.nn.relu(jnp.dot(second, bottom_third, preferred_element_type=F32) + bias_third)
    padded = jnp.concatenate([top_hidden, jnp.zeros((1, top_hidden.shape[1]), BF)], axis=0)
    weights = jnp.take(padded, jnp.asarray(FEATURE_ROWS), axis=0)
    last = jnp.broadcast_to(top_logit.reshape(1, -1), (8, top_logit.shape[0]))
    last_bias = jnp.broadcast_to(bias_logit[None, :], (1, 128))
    outgoing, weights, bottom, last, last_bias = lax.optimization_barrier(
        (outgoing, weights, bottom, last, last_bias)
    )
    rehomed = exchange(outgoing, "chip")
    logits, term = tail(
        arrived,
        jnp.asarray(labels_by_holder()),
        bottom,
        weights,
        bias_hidden[None, :],
        last,
        last_bias,
        labels[None, :],
    )
    term = ring_sum(term, "hst")
    term = term + lax.ppermute(term, "chip", [(i, i ^ 1) for i in range(chips)])
    for step, hop in ((2, 0), (2, 1), (8, 0)):
        term = near_hop(term, "chip", chips, step, hop)
    rehomed, term = lax.optimization_barrier((keep(rehomed), term))
    term = near_hop(term, "chip", chips, 8, 1)
    return rehomed, logits[0], term[0, 0]


def solution(mesh):
    split = P(ALL)
    return jax.shard_map(
        per_device,
        mesh=mesh,
        in_specs=(split,) * 11 + (P(),) * 10,
        out_specs=(split, split, P()),
        check_vma=False,
    )
```

```python
import functools

import jax
import jax.numpy as jnp
import numpy as np
from jax import lax
from jax.experimental import pallas as pl
from jax.experimental.pallas import tpu as pltpu
from jax.sharding import PartitionSpec as P

ALL = ("hst", "chip")
PERIOD = 13
HOME, ORPHAN = 48, 32
FIXED = 6
SLOTS = 84
ROWS = 88
F = 26
BATCH = 512
NONE = 1023
QW = 896
BF, F32 = jnp.bfloat16, jnp.float32
VMEM = pl.BlockSpec(memory_space=pltpu.VMEM)
SMEM = pl.BlockSpec(memory_space=pltpu.SMEM)


def slot_tables():
    table = np.full((PERIOD, 128), -1, np.int32)
    label = np.full((PERIOD, 3), -1, np.int32)
    for r in range(PERIOD):
        for g in range(PERIOD):
            k = (g - 11 * r) % PERIOD
            o = (g - 4 - 3 * r) % PERIOD
            for e in range(2):
                table[r, FIXED * g + e] = 2 * k + e
                if k + PERIOD < HOME // 2:
                    table[r, FIXED * g + 2 + e] = 2 * (k + PERIOD) + e
                table[r, FIXED * g + 4 + e] = 2 * o + e
        rest = [(PERIOD + i, (4 + 3 * r + i) % PERIOD) for i in range(3)]
        free = [0, 1, 2]
        for k, g in sorted(rest, key=lambda item: item[1] == 0):
            at = g % 3 if g % 3 in free else free[0]
            free.remove(at)
            label[r, at] = g
            for e in range(2):
                table[r, PERIOD * FIXED + 2 * at + e] = 2 * k + e
    for g in range(1, PERIOD):
        assert all(at == g % 3 for r in range(PERIOD) for at in range(3) if label[r, at] == g)
    return table, label


def feature_rows():
    rows = np.full((QW,), 479, np.int32)
    rows[:128] = np.arange(128)
    at = 128
    for a in range(4):
        for tile in range(1 if a < 2 else 2):
            for lane in range(128):
                turn = (lane - 7) % 128
                i, j = 8 * a + turn % 8, 16 * tile + turn // 8
                if j < i <= F:
                    rows[at + lane] = 128 + i * (i - 1) // 2 + j
            at += 128
    return rows


TABLE, LABEL = slot_tables()
FEATURE_ROWS = feature_rows()


def route_kernel(owner, orphans, out, count):
    slots = out.shape[0] // count.shape[0]

    def clear(c, _):
        count[c] = 0
        return 0

    lax.fori_loop(0, count.shape[0], clear, 0)
    out[...] = jnp.zeros_like(out)

    def place(i, _):
        o = owner[i]
        n = count[o]
        out[slots * o + n] = orphans[i]
        count[o] = n + 1
        return 0

    lax.fori_loop(0, orphans.shape[0], place, 0)


def route(orphan_owner, orphans, chips):
    return pl.pallas_call(
        route_kernel,
        out_shape=jax.ShapeDtypeStruct((2 * chips,) + orphans.shape[1:], BF),
        in_specs=[SMEM, VMEM],
        out_specs=VMEM,
        scratch_shapes=[pltpu.SMEM((chips,), jnp.int32)],
        compiler_params=pltpu.CompilerParams(vmem_limit_bytes=16 << 20),
        cost_estimate=pl.CostEstimate(flops=0, transcendentals=0, bytes_accessed=3 << 20),
    )(orphan_owner, orphans)


def pool_kernel(*refs):
    given, out, (wide, sam, ready), held, sem, sent = refs[:8], refs[8], refs[9:12], refs[12:20], refs[20], refs[21]
    cuts = [(n, None) for n in range(2, 8)] + [(0, (0, 12)), (0, (26, 38)), (1, (0, 12))]
    cuts = [cuts, [(0, (12, 26)), (0, (38, 48)), (1, (12, 32))]]
    waves = []
    for wave in cuts:
        copies = []
        for n, cut in wave:
            at = pl.ds(cut[0], cut[1] - cut[0]) if cut else pl.ds(0, given[n].shape[0])
            number = len(copies) + 9 * len(waves)
            copies.append(pltpu.make_async_copy(given[n].at[at], held[n].at[at], sem.at[number]))
            copies[-1].start()
        waves.append(copies)
    home, orphan = (held[0],) + tuple(held[2:5]), (held[1],) + tuple(held[5:8])
    me = lax.axis_index("hst") * lax.axis_size("chip") + lax.axis_index("chip")
    rows = lax.broadcasted_iota(jnp.int32, (128, 128), 0).astype(F32).astype(BF)
    place = lax.broadcasted_iota(jnp.int32, (8, 128), 0)
    one, zero = jnp.ones((), BF), jnp.zeros((), BF)
    sam[...] = jnp.full(sam.shape, NONE, jnp.int32)
    for s in range(SLOTS + 2, ROWS):
        wide[pl.ds(s, 128, stride=ROWS), :] = jnp.zeros((128, 128), F32)
    for copy in waves[0]:
        copy.wait()

    def piece(slot, b, blocks, off, length, samples):
        live = jnp.where(place < length[pl.ds(b, 1), :], off[b], -1).astype(F32).astype(BF)
        counts = jnp.zeros((128, 128), BF)
        for n in range(8):
            counts = counts + jnp.where(rows == live[n : n + 1, :], one, zero)
        sums = lax.dot_general(counts, blocks[b], (((0,), (0,)), ((), ())), preferred_element_type=F32)
        wide[pl.ds(slot, 128, stride=ROWS), :] = sums
        sam[pl.ds(slot, 1), :] = samples[pl.ds(b, 1), :]

    def pair(k, more):
        g = FIXED * lax.rem(11 * me + k, PERIOD)
        for e in range(2):
            piece(g + e, 2 * k + e, *home)
        for e in range(2):
            if more:
                piece(g + 2 + e, 2 * (k + PERIOD) + e, *home)
            else:
                wide[pl.ds(g + 2 + e, 128, stride=ROWS), :] = jnp.zeros((128, 128), F32)
        g = FIXED * lax.rem(4 + 3 * me + k, PERIOD)
        for e in range(2):
            piece(g + 4 + e, 2 * k + e, *orphan)

    def step(k, _):
        pair(k, True)
        return 0

    both = HOME // 2 - PERIOD
    lax.fori_loop(0, 6, step, 0, unroll=3)
    for copy in waves[1]:
        copy.wait()
    lax.fori_loop(6, both, step, 0, unroll=5)
    for k in range(both, PERIOD):
        pair(k, False)
    rest = [lax.rem(4 + 3 * me + i, PERIOD) for i in range(3)]
    for i, g in enumerate(rest):
        others = sum(lax.rem(h, 3) for h in rest if h is not g)
        at = jnp.where(g == 0, 3 - others, lax.rem(g, 3))
        for e in range(2):
            piece(PERIOD * FIXED + 2 * at + e, 2 * (PERIOD + i) + e, *orphan)
    index = sam[...]
    wide[pl.ds(SLOTS, 128, stride=ROWS), :] = (index >> 4).astype(F32).T
    wide[pl.ds(SLOTS + 1, 128, stride=ROWS), :] = (index & 15).astype(F32).T

    parts = sent.shape[0]
    span = 128 // parts
    copies = []
    for n in range(parts):

        def narrow(q, _):
            q = span // 4 * n + q
            ready[pl.ds(4 * q, 4)] = wide[pl.ds(4 * q * ROWS, 4 * ROWS), :].reshape(4, ROWS, 128).astype(BF)
            return 0

        lax.fori_loop(0, span // 4, narrow, 0, unroll=2)
        at = pl.ds(span * n, span)
        copies.append(pltpu.make_async_copy(ready.at[at], out.at[at], sent.at[n]))
        copies[-1].start()
    for copy in copies:
        copy.wait()


def pool(*arrays):
    return pl.pallas_call(
        pool_kernel,
        out_shape=jax.ShapeDtypeStruct((128, ROWS, 128), BF),
        in_specs=[pl.BlockSpec(memory_space=pl.ANY)] * 8,
        out_specs=pl.BlockSpec(memory_space=pl.ANY),
        scratch_shapes=[
            pltpu.VMEM((128 * ROWS, 128), F32),
            pltpu.VMEM((128, 128), jnp.int32),
            pltpu.VMEM((128, ROWS, 128), BF),
        ]
        + [pltpu.VMEM(a.shape, a.dtype) for a in arrays]
        + [pltpu.SemaphoreType.DMA((12,)), pltpu.SemaphoreType.DMA((4,))],
        compiler_params=pltpu.CompilerParams(vmem_limit_bytes=60 << 20),
        cost_estimate=pl.CostEstimate(flops=84 * 128 * 128 * 256, transcendentals=0, bytes_accessed=6 << 20),
    )(*arrays)


def tail_kernel(*refs):
    (given, *others), (logits, loss), refs = refs[:8], refs[8:10], refs[10:]
    recv, (label, bottom, weights, bias, last, last_bias, marks), refs = refs[0], refs[1:8], refs[8:]
    wide, hi, lo, stack, packed, came, sems = refs
    parts = came.shape[0]
    span = 128 // parts
    copies = []
    for n in range(parts):
        at = pl.ds(span * n, span)
        copies.append(pltpu.make_async_copy(given.at[at], recv.at[at], came.at[n]))
        copies[-1].start()
    held = (label, bottom, weights, bias, last, last_bias, marks)
    fetches = [pltpu.make_async_copy(g, h, sems.at[n]) for n, (g, h) in enumerate(zip(others, held))]
    for fetch in fetches:
        fetch.start()
    zero = jnp.zeros((), BF)
    ones = lax.broadcasted_iota(jnp.int32, (16, 128), 0).astype(F32).astype(BF)

    def widen(p, _):
        wide[pl.ds(4 * p * ROWS, 4 * ROWS), :] = recv[pl.ds(4 * p, 4)].astype(F32).reshape(4 * ROWS, 128)
        return 0

    for n in range(parts):
        copies[n].wait()
        lax.fori_loop(span // 4 * n, span // 4 * (n + 1), widen, 0, unroll=2)
    hi[...] = wide[pl.ds(SLOTS, 128, stride=ROWS), :].T
    lo[...] = wide[pl.ds(SLOTS + 1, 128, stride=ROWS), :].T

    for fetch in fetches[:2]:
        fetch.wait()
    stack[0] = bottom[...].astype(BF).astype(F32)

    def hits(slot, keep=None):
        high = hi[pl.ds(slot, 1), :]
        if keep is not None:
            high = jnp.where(keep, high, 63.0)
        high = jnp.broadcast_to(high, (16, 128)).astype(BF)
        low = jnp.broadcast_to(lo[pl.ds(slot, 1), :], (16, 128)).astype(BF)
        low = jnp.where(low == ones, jnp.ones((), BF), zero)
        return jnp.concatenate([jnp.where(high == jnp.asarray(h, BF), low, zero) for h in range(32)], axis=0)

    def rows(slot):
        return wide[pl.ds(slot, 128, stride=ROWS), :].astype(BF)

    def pooled(g, places):
        for e in range(2):
            slots = [(FIXED * g + 2 * n + e, None) for n in range(3)]
            for at in places:
                keep = label[pl.ds(at, 1), :] == jnp.asarray(g, jnp.int32)
                slots.append((PERIOD * FIXED + 2 * at + e, keep))
            left = jnp.concatenate([hits(s, keep) for s, keep in slots], axis=1)
            right = jnp.concatenate([rows(s) for s, _ in slots], axis=0)
            total = jnp.dot(left, right, preferred_element_type=F32)
            stack[1 + 2 * g + e] = total.astype(BF).astype(F32)

    pooled(0, [0, 1, 2])

    def group(g, _):
        pooled(g, [lax.rem(g, 3)])
        return 0

    lax.fori_loop(1, PERIOD, group, 0, unroll=4)

    packed[:, :128] = bottom[...].astype(BF)
    own = lax.broadcasted_iota(jnp.int32, (8, 128), 1) % 8 == 7 - lax.broadcasted_iota(jnp.int32, (8, 128), 0)

    back = 7 - lax.broadcasted_iota(jnp.int32, (8, 128), 0)

    def interact(m, _):
        halves = []
        for half in range(2):
            left = stack[:, pl.ds(16 * m + 8 * half, 8), :].reshape(8 * (F + 1), 128).astype(BF)
            right = [jnp.take_along_axis(stack[j, pl.ds(16 * m + 8 * half, 8), :], back, axis=0) for j in range(F + 1)]
            right = jnp.concatenate(right + [jnp.zeros((8 * (31 - F), 128), F32)], axis=0).astype(BF)
            gram = lax.dot_general(left, right, (((1,), (1,)), ((), ())), preferred_element_type=F32)
            columns = []
            for a in range(4):
                for tile in range(1 if a < 2 else 2):
                    total = None
                    for c in range(8):
                        i = 8 * a + c
                        if i > F or 16 * tile >= i:
                            continue
                        part = jnp.where(own, gram[8 * i : 8 * i + 8, 128 * tile : 128 * tile + 128], 0.0)
                        part = pltpu.roll(part, c, 1, stride=1, stride_axis=0)
                        total = part if total is None else total + part
                    columns.append(total)
            halves.append(jnp.concatenate(columns, axis=1))
        packed[pl.ds(pl.multiple_of(16 * m, 16), 16), 128:] = jnp.concatenate(halves, axis=0).astype(BF)
        return 0

    lax.fori_loop(0, BATCH // 16, interact, 0, unroll=8)

    for fetch in fetches[2:]:
        fetch.wait()
    hidden = jnp.dot(packed[...], weights[...], preferred_element_type=F32)
    hidden = jnp.maximum(hidden + bias[...], 0.0).astype(BF)
    out = lax.dot_general(last[...], hidden, (((1,), (1,)), ((), ())), preferred_element_type=F32)
    x = out[:1] + last_bias[:, :1]
    logits[...] = x
    soft = jnp.maximum(x, 0.0) + jnp.log1p(jnp.exp(-jnp.abs(x)))
    term = jnp.sum(soft - marks[...].astype(F32) * x)
    loss[...] = jnp.full(loss.shape, term, F32)


def tail(given, *others):
    anywhere = pl.BlockSpec(memory_space=pl.ANY)
    return pl.pallas_call(
        tail_kernel,
        out_shape=(jax.ShapeDtypeStruct((1, BATCH), F32), jax.ShapeDtypeStruct((1, 128), F32)),
        in_specs=[anywhere] * 8,
        out_specs=(VMEM, VMEM),
        scratch_shapes=[pltpu.VMEM(a.shape, a.dtype) for a in (given,) + others]
        + [
            pltpu.VMEM((128 * ROWS, 128), F32),
            pltpu.VMEM((128, 128), F32),
            pltpu.VMEM((128, 128), F32),
            pltpu.VMEM((F + 1, BATCH, 128), F32),
            pltpu.VMEM((BATCH, QW), BF),
            pltpu.SemaphoreType.DMA((4,)),
            pltpu.SemaphoreType.DMA((7,)),
        ],
        compiler_params=pltpu.CompilerParams(vmem_limit_bytes=60 << 20),
        cost_estimate=pl.CostEstimate(flops=6 << 30, transcendentals=0, bytes_accessed=5 << 20),
    )(given, *others)


def labels_by_holder():
    label = np.full((8, 128), -1, np.int32)
    label[:3] = LABEL[np.arange(128) % PERIOD].T
    return label


def exchange(value, axes):
    return lax.all_to_all(value, axes, split_axis=0, concat_axis=0, tiled=True)


def swap_sum(value, axis, step):
    return value + lax.ppermute(value, axis, [(i, i ^ step) for i in range(lax.axis_size(axis))])


def keep_kernel(given, out, sent):
    span = given.shape[0] // sent.shape[0]
    copies = []
    for n in range(sent.shape[0]):
        at = pl.ds(span * n, span)
        copies.append(pltpu.make_async_copy(given.at[at], out.at[at], sent.at[n]))
        copies[-1].start()
    for copy in copies:
        copy.wait()


def keep(value):
    return pl.pallas_call(
        keep_kernel,
        out_shape=jax.ShapeDtypeStruct(value.shape, value.dtype),
        in_specs=[VMEM],
        out_specs=pl.BlockSpec(memory_space=pl.ANY),
        scratch_shapes=[pltpu.SemaphoreType.DMA((8,))],
        compiler_params=pltpu.CompilerParams(vmem_limit_bytes=8 << 20),
        cost_estimate=pl.CostEstimate(flops=0, transcendentals=0, bytes_accessed=4 << 20),
    )(value)


def per_device(
    resident_row_blocks,
    orphan_blocks,
    home_offsets,
    home_lengths,
    home_samples,
    orphan_offsets,
    orphan_lengths,
    orphan_samples,
    orphan_owner,
    dense_inputs,
    labels,
    bottom_first,
    bias_first,
    bottom_second,
    bias_second,
    bottom_third,
    bias_third,
    top_hidden,
    bias_hidden,
    top_logit,
    bias_logit,
):
    chips = lax.axis_size("chip")
    outgoing = route(orphan_owner[:, 0], orphan_blocks, chips)
    pieces = pool(
        resident_row_blocks,
        orphan_blocks,
        home_offsets.transpose(0, 2, 1),
        home_lengths,
        home_samples,
        orphan_offsets.transpose(0, 2, 1),
        orphan_lengths,
        orphan_samples,
    )
    arrived = exchange(pieces, ALL)
    first = jax.nn.relu(
        jnp.dot(dense_inputs, bottom_first, preferred_element_type=F32) + bias_first
    ).astype(BF)
    second = jax.nn.relu(
        jnp.dot(first, bottom_second, preferred_element_type=F32) + bias_second
    ).astype(BF)
    bottom = jax.nn.relu(jnp.dot(second, bottom_third, preferred_element_type=F32) + bias_third)
    padded = jnp.concatenate([top_hidden, jnp.zeros((1, top_hidden.shape[1]), BF)], axis=0)
    weights = jnp.take(padded, jnp.asarray(FEATURE_ROWS), axis=0)
    last = jnp.broadcast_to(top_logit.reshape(1, -1), (8, top_logit.shape[0]))
    last_bias = jnp.broadcast_to(bias_logit[None, :], (1, 128))
    outgoing, weights, bottom, last, last_bias = lax.optimization_barrier(
        (outgoing, weights, bottom, last, last_bias)
    )
    rehomed = exchange(outgoing, "chip")
    logits, term = tail(
        arrived,
        jnp.asarray(labels_by_holder()),
        bottom,
        weights,
        bias_hidden[None, :],
        last,
        last_bias,
        labels[None, :],
    )
    for axis, step in (("hst", 1), ("hst", 2), ("chip", 1), ("chip", 8), ("chip", 16), ("chip", 2)):
        term = swap_sum(term, axis, step)
    rehomed, term = lax.optimization_barrier((keep(rehomed), term))
    term = swap_sum(term, "chip", 4)
    return rehomed, logits[0], term[0, 0]


def solution(mesh):
    split = P(ALL)
    return jax.shard_map(
        per_device,
        mesh=mesh,
        in_specs=(split,) * 11 + (P(),) * 10,
        out_specs=(split, split, P()),
        check_vma=False,
    )
```

```python
import functools

import jax
import jax.numpy as jnp
import numpy as np
from jax import lax
from jax.experimental import pallas as pl
from jax.experimental.pallas import tpu as pltpu
from jax.sharding import PartitionSpec as P

ALL = ("hst", "chip")
PERIOD = 13
HOME, ORPHAN = 48, 32
FIXED = 6
SLOTS = 84
ROWS = 88
F = 26
BATCH = 512
NONE = 1023
QW = 896
BF, F32 = jnp.bfloat16, jnp.float32
VMEM = pl.BlockSpec(memory_space=pltpu.VMEM)
SMEM = pl.BlockSpec(memory_space=pltpu.SMEM)


def slot_tables():
    table = np.full((PERIOD, 128), -1, np.int32)
    label = np.full((PERIOD, 3), -1, np.int32)
    for r in range(PERIOD):
        for g in range(PERIOD):
            k = (g - 11 * r) % PERIOD
            o = (g - 4 - 3 * r) % PERIOD
            for e in range(2):
                table[r, FIXED * g + e] = 2 * k + e
                if k + PERIOD < HOME // 2:
                    table[r, FIXED * g + 2 + e] = 2 * (k + PERIOD) + e
                table[r, FIXED * g + 4 + e] = 2 * o + e
        rest = [(PERIOD + i, (4 + 3 * r + i) % PERIOD) for i in range(3)]
        free = [0, 1, 2]
        for k, g in sorted(rest, key=lambda item: item[1] == 0):
            at = g % 3 if g % 3 in free else free[0]
            free.remove(at)
            label[r, at] = g
            for e in range(2):
                table[r, PERIOD * FIXED + 2 * at + e] = 2 * k + e
    for g in range(1, PERIOD):
        assert all(at == g % 3 for r in range(PERIOD) for at in range(3) if label[r, at] == g)
    return table, label


def feature_rows():
    rows = np.full((QW,), 479, np.int32)
    rows[:128] = np.arange(128)
    at = 128
    for a in range(4):
        for tile in range(1 if a < 2 else 2):
            for lane in range(128):
                turn = (lane - 7) % 128
                i, j = 8 * a + turn % 8, 16 * tile + turn // 8
                if j < i <= F:
                    rows[at + lane] = 128 + i * (i - 1) // 2 + j
            at += 128
    return rows


TABLE, LABEL = slot_tables()
FEATURE_ROWS = feature_rows()


def route_kernel(owner, orphans, out, count):
    slots = out.shape[0] // count.shape[0]

    def clear(c, _):
        count[c] = 0
        return 0

    lax.fori_loop(0, count.shape[0], clear, 0)
    out[...] = jnp.zeros_like(out)

    def place(i, _):
        o = owner[i]
        n = count[o]
        out[slots * o + n] = orphans[i]
        count[o] = n + 1
        return 0

    lax.fori_loop(0, orphans.shape[0], place, 0)


def route(orphan_owner, orphans, chips):
    return pl.pallas_call(
        route_kernel,
        out_shape=jax.ShapeDtypeStruct((2 * chips,) + orphans.shape[1:], BF),
        in_specs=[SMEM, VMEM],
        out_specs=VMEM,
        scratch_shapes=[pltpu.SMEM((chips,), jnp.int32)],
        compiler_params=pltpu.CompilerParams(vmem_limit_bytes=16 << 20),
        cost_estimate=pl.CostEstimate(flops=0, transcendentals=0, bytes_accessed=3 << 20),
    )(orphan_owner, orphans)


def pool_kernel(*refs):
    given, out, (wide, sam, ready), held, sem, sent = refs[:8], refs[8], refs[9:12], refs[12:20], refs[20], refs[21]
    cuts = [(n, None) for n in range(2, 8)] + [(0, (0, 12)), (0, (26, 38)), (1, (0, 12))]
    cuts = [cuts, [(0, (12, 26)), (0, (38, 48)), (1, (12, 32))]]
    waves = []
    for wave in cuts:
        copies = []
        for n, cut in wave:
            at = pl.ds(cut[0], cut[1] - cut[0]) if cut else pl.ds(0, given[n].shape[0])
            number = len(copies) + 9 * len(waves)
            copies.append(pltpu.make_async_copy(given[n].at[at], held[n].at[at], sem.at[number]))
            copies[-1].start()
        waves.append(copies)
    home, orphan = (held[0],) + tuple(held[2:5]), (held[1],) + tuple(held[5:8])
    me = lax.axis_index("hst") * lax.axis_size("chip") + lax.axis_index("chip")
    rows = lax.broadcasted_iota(jnp.int32, (128, 128), 0).astype(F32).astype(BF)
    place = lax.broadcasted_iota(jnp.int32, (8, 128), 0)
    one, zero = jnp.ones((), BF), jnp.zeros((), BF)
    sam[...] = jnp.full(sam.shape, NONE, jnp.int32)
    for s in range(SLOTS + 2, ROWS):
        wide[pl.ds(s, 128, stride=ROWS), :] = jnp.zeros((128, 128), F32)
    for copy in waves[0]:
        copy.wait()

    def piece(slot, b, blocks, off, length, samples):
        live = jnp.where(place < length[pl.ds(b, 1), :], off[b], -1).astype(F32).astype(BF)
        counts = jnp.zeros((128, 128), BF)
        for n in range(8):
            counts = counts + jnp.where(rows == live[n : n + 1, :], one, zero)
        sums = lax.dot_general(counts, blocks[b], (((0,), (0,)), ((), ())), preferred_element_type=F32)
        wide[pl.ds(slot, 128, stride=ROWS), :] = sums
        sam[pl.ds(slot, 1), :] = samples[pl.ds(b, 1), :]

    def pair(k, more):
        g = FIXED * lax.rem(11 * me + k, PERIOD)
        for e in range(2):
            piece(g + e, 2 * k + e, *home)
        for e in range(2):
            if more:
                piece(g + 2 + e, 2 * (k + PERIOD) + e, *home)
            else:
                wide[pl.ds(g + 2 + e, 128, stride=ROWS), :] = jnp.zeros((128, 128), F32)
        g = FIXED * lax.rem(4 + 3 * me + k, PERIOD)
        for e in range(2):
            piece(g + 4 + e, 2 * k + e, *orphan)

    def step(k, _):
        pair(k, True)
        return 0

    both = HOME // 2 - PERIOD
    lax.fori_loop(0, 6, step, 0, unroll=6)
    for copy in waves[1]:
        copy.wait()
    lax.fori_loop(6, both, step, 0, unroll=5)
    for k in range(both, PERIOD):
        pair(k, False)
    rest = [lax.rem(4 + 3 * me + i, PERIOD) for i in range(3)]
    for i, g in enumerate(rest):
        others = sum(lax.rem(h, 3) for h in rest if h is not g)
        at = jnp.where(g == 0, 3 - others, lax.rem(g, 3))
        for e in range(2):
            piece(PERIOD * FIXED + 2 * at + e, 2 * (PERIOD + i) + e, *orphan)
    index = sam[...]
    wide[pl.ds(SLOTS, 128, stride=ROWS), :] = (index >> 4).astype(F32).T
    wide[pl.ds(SLOTS + 1, 128, stride=ROWS), :] = (index & 15).astype(F32).T

    parts = sent.shape[0]
    span = 128 // parts
    copies = []
    for n in range(parts):

        def narrow(q, _):
            q = span // 4 * n + q
            ready[pl.ds(4 * q, 4)] = wide[pl.ds(4 * q * ROWS, 4 * ROWS), :].reshape(4, ROWS, 128).astype(BF)
            return 0

        lax.fori_loop(0, span // 4, narrow, 0, unroll=2)
        at = pl.ds(span * n, span)
        copies.append(pltpu.make_async_copy(ready.at[at], out.at[at], sent.at[n]))
        copies[-1].start()
    for copy in copies:
        copy.wait()


def pool(*arrays):
    return pl.pallas_call(
        pool_kernel,
        out_shape=jax.ShapeDtypeStruct((128, ROWS, 128), BF),
        in_specs=[pl.BlockSpec(memory_space=pl.ANY)] * 8,
        out_specs=pl.BlockSpec(memory_space=pl.ANY),
        scratch_shapes=[
            pltpu.VMEM((128 * ROWS, 128), F32),
            pltpu.VMEM((128, 128), jnp.int32),
            pltpu.VMEM((128, ROWS, 128), BF),
        ]
        + [pltpu.VMEM(a.shape, a.dtype) for a in arrays]
        + [pltpu.SemaphoreType.DMA((12,)), pltpu.SemaphoreType.DMA((8,))],
        compiler_params=pltpu.CompilerParams(vmem_limit_bytes=60 << 20),
        cost_estimate=pl.CostEstimate(flops=84 * 128 * 128 * 256, transcendentals=0, bytes_accessed=6 << 20),
    )(*arrays)


def tail_kernel(*refs):
    (given, *others), (logits, loss), refs = refs[:8], refs[8:10], refs[10:]
    recv, (label, bottom, weights, bias, last, last_bias, marks), refs = refs[0], refs[1:8], refs[8:]
    wide, hi, lo, stack, packed, came, sems = refs
    parts = came.shape[0]
    span = 128 // parts
    copies = []
    for n in range(parts):
        at = pl.ds(span * n, span)
        copies.append(pltpu.make_async_copy(given.at[at], recv.at[at], came.at[n]))
        copies[-1].start()
    held = (label, bottom, weights, bias, last, last_bias, marks)
    fetches = [pltpu.make_async_copy(g, h, sems.at[n]) for n, (g, h) in enumerate(zip(others, held))]
    for fetch in fetches:
        fetch.start()
    zero = jnp.zeros((), BF)
    ones = lax.broadcasted_iota(jnp.int32, (16, 128), 0).astype(F32).astype(BF)

    def widen(p, _):
        wide[pl.ds(4 * p * ROWS, 4 * ROWS), :] = recv[pl.ds(4 * p, 4)].astype(F32).reshape(4 * ROWS, 128)
        return 0

    for n in range(parts):
        copies[n].wait()
        lax.fori_loop(span // 4 * n, span // 4 * (n + 1), widen, 0, unroll=2)
    hi[...] = wide[pl.ds(SLOTS, 128, stride=ROWS), :].T
    lo[...] = wide[pl.ds(SLOTS + 1, 128, stride=ROWS), :].T

    for fetch in fetches[:2]:
        fetch.wait()
    stack[0] = bottom[...].astype(BF).astype(F32)

    def hits(slot, keep=None):
        high = hi[pl.ds(slot, 1), :]
        if keep is not None:
            high = jnp.where(keep, high, 63.0)
        high = jnp.broadcast_to(high, (16, 128)).astype(BF)
        low = jnp.broadcast_to(lo[pl.ds(slot, 1), :], (16, 128)).astype(BF)
        low = jnp.where(low == ones, jnp.ones((), BF), zero)
        return jnp.concatenate([jnp.where(high == jnp.asarray(h, BF), low, zero) for h in range(32)], axis=0)

    def rows(slot):
        return wide[pl.ds(slot, 128, stride=ROWS), :].astype(BF)

    def pooled(g, places):
        for e in range(2):
            slots = [(FIXED * g + 2 * n + e, None) for n in range(3)]
            for at in places:
                keep = label[pl.ds(at, 1), :] == jnp.asarray(g, jnp.int32)
                slots.append((PERIOD * FIXED + 2 * at + e, keep))
            left = jnp.concatenate([hits(s, keep) for s, keep in slots], axis=1)
            right = jnp.concatenate([rows(s) for s, _ in slots], axis=0)
            total = jnp.dot(left, right, preferred_element_type=F32)
            stack[1 + 2 * g + e] = total.astype(BF).astype(F32)

    pooled(0, [0, 1, 2])

    def group(g, _):
        pooled(g, [lax.rem(g, 3)])
        return 0

    lax.fori_loop(1, PERIOD, group, 0, unroll=4)

    packed[:, :128] = bottom[...].astype(BF)
    own = lax.broadcasted_iota(jnp.int32, (8, 128), 1) % 8 == 7 - lax.broadcasted_iota(jnp.int32, (8, 128), 0)

    back = 7 - lax.broadcasted_iota(jnp.int32, (8, 128), 0)

    def interact(m, _):
        halves = []
        for half in range(2):
            left = stack[:, pl.ds(16 * m + 8 * half, 8), :].reshape(8 * (F + 1), 128).astype(BF)
            right = [jnp.take_along_axis(stack[j, pl.ds(16 * m + 8 * half, 8), :], back, axis=0) for j in range(F + 1)]
            right = jnp.concatenate(right + [jnp.zeros((8 * (31 - F), 128), F32)], axis=0).astype(BF)
            gram = lax.dot_general(left, right, (((1,), (1,)), ((), ())), preferred_element_type=F32)
            columns = []
            for a in range(4):
                for tile in range(1 if a < 2 else 2):
                    total = None
                    for c in range(8):
                        i = 8 * a + c
                        if i > F or 16 * tile >= i:
                            continue
                        part = jnp.where(own, gram[8 * i : 8 * i + 8, 128 * tile : 128 * tile + 128], 0.0)
                        part = pltpu.roll(part, c, 1, stride=1, stride_axis=0)
                        total = part if total is None else total + part
                    columns.append(total)
            halves.append(jnp.concatenate(columns, axis=1))
        packed[pl.ds(pl.multiple_of(16 * m, 16), 16), 128:] = jnp.concatenate(halves, axis=0).astype(BF)
        return 0

    lax.fori_loop(0, BATCH // 16, interact, 0, unroll=8)

    for fetch in fetches[2:]:
        fetch.wait()
    hidden = jnp.dot(packed[...], weights[...], preferred_element_type=F32)
    hidden = jnp.maximum(hidden + bias[...], 0.0).astype(BF)
    out = lax.dot_general(last[...], hidden, (((1,), (1,)), ((), ())), preferred_element_type=F32)
    x = out[:1] + last_bias[:, :1]
    logits[...] = x
    soft = jnp.maximum(x, 0.0) + jnp.log1p(jnp.exp(-jnp.abs(x)))
    term = jnp.sum(soft - marks[...].astype(F32) * x)
    loss[...] = jnp.full(loss.shape, term, F32)


def tail(given, *others):
    anywhere = pl.BlockSpec(memory_space=pl.ANY)
    return pl.pallas_call(
        tail_kernel,
        out_shape=(jax.ShapeDtypeStruct((1, BATCH), F32), jax.ShapeDtypeStruct((1, 128), F32)),
        in_specs=[anywhere] * 8,
        out_specs=(VMEM, VMEM),
        scratch_shapes=[pltpu.VMEM(a.shape, a.dtype) for a in (given,) + others]
        + [
            pltpu.VMEM((128 * ROWS, 128), F32),
            pltpu.VMEM((128, 128), F32),
            pltpu.VMEM((128, 128), F32),
            pltpu.VMEM((F + 1, BATCH, 128), F32),
            pltpu.VMEM((BATCH, QW), BF),
            pltpu.SemaphoreType.DMA((8,)),
            pltpu.SemaphoreType.DMA((7,)),
        ],
        compiler_params=pltpu.CompilerParams(vmem_limit_bytes=60 << 20),
        cost_estimate=pl.CostEstimate(flops=6 << 30, transcendentals=0, bytes_accessed=5 << 20),
    )(given, *others)


def labels_by_holder():
    label = np.full((8, 128), -1, np.int32)
    label[:3] = LABEL[np.arange(128) % PERIOD].T
    return label


def exchange(value, axes):
    return lax.all_to_all(value, axes, split_axis=0, concat_axis=0, tiled=True)


def ring_sum(value, axis):
    one, two, three = (lax.ppermute(value, axis, [(i, (i + k) % 4) for i in range(4)]) for k in (1, 2, 3))
    return (value + two) + (one + three)


def part_ring(value, axis, size, step):
    one, two, three = (
        lax.ppermute(value, axis, [(i, i - i // step % 4 * step + (i // step + k) % 4 * step) for i in range(size)])
        for k in (1, 2, 3)
    )
    return (value + two) + (one + three)


def keep_kernel(given, out, sent):
    span = given.shape[0] // sent.shape[0]
    copies = []
    for n in range(sent.shape[0]):
        at = pl.ds(span * n, span)
        copies.append(pltpu.make_async_copy(given.at[at], out.at[at], sent.at[n]))
        copies[-1].start()
    for copy in copies:
        copy.wait()


def keep(value):
    return pl.pallas_call(
        keep_kernel,
        out_shape=jax.ShapeDtypeStruct(value.shape, value.dtype),
        in_specs=[VMEM],
        out_specs=pl.BlockSpec(memory_space=pl.ANY),
        scratch_shapes=[pltpu.SemaphoreType.DMA((8,))],
        compiler_params=pltpu.CompilerParams(vmem_limit_bytes=8 << 20),
        cost_estimate=pl.CostEstimate(flops=0, transcendentals=0, bytes_accessed=4 << 20),
    )(value)


def per_device(
    resident_row_blocks,
    orphan_blocks,
    home_offsets,
    home_lengths,
    home_samples,
    orphan_offsets,
    orphan_lengths,
    orphan_samples,
    orphan_owner,
    dense_inputs,
    labels,
    bottom_first,
    bias_first,
    bottom_second,
    bias_second,
    bottom_third,
    bias_third,
    top_hidden,
    bias_hidden,
    top_logit,
    bias_logit,
):
    chips = lax.axis_size("chip")
    outgoing = route(orphan_owner[:, 0], orphan_blocks, chips)
    pieces = pool(
        resident_row_blocks,
        orphan_blocks,
        home_offsets.transpose(0, 2, 1),
        home_lengths,
        home_samples,
        orphan_offsets.transpose(0, 2, 1),
        orphan_lengths,
        orphan_samples,
    )
    arrived = exchange(pieces, ALL)
    first = jax.nn.relu(
        jnp.dot(dense_inputs, bottom_first, preferred_element_type=F32) + bias_first
    ).astype(BF)
    second = jax.nn.relu(
        jnp.dot(first, bottom_second, preferred_element_type=F32) + bias_second
    ).astype(BF)
    bottom = jax.nn.relu(jnp.dot(second, bottom_third, preferred_element_type=F32) + bias_third)
    padded = jnp.concatenate([top_hidden, jnp.zeros((1, top_hidden.shape[1]), BF)], axis=0)
    weights = jnp.take(padded, jnp.asarray(FEATURE_ROWS), axis=0)
    last = jnp.broadcast_to(top_logit.reshape(1, -1), (8, top_logit.shape[0]))
    last_bias = jnp.broadcast_to(bias_logit[None, :], (1, 128))
    outgoing, weights, bottom, last, last_bias = lax.optimization_barrier(
        (outgoing, weights, bottom, last, last_bias)
    )
    rehomed = exchange(outgoing, "chip")
    logits, term = tail(
        arrived,
        jnp.asarray(labels_by_holder()),
        bottom,
        weights,
        bias_hidden[None, :],
        last,
        last_bias,
        labels[None, :],
    )
    term = ring_sum(term, "hst")
    term = term + lax.ppermute(term, "chip", [(i, i ^ 1) for i in range(chips)])
    term = part_ring(term, "chip", chips, 2)
    rehomed, term = lax.optimization_barrier((keep(rehomed), term))
    term = part_ring(term, "chip", chips, 8)
    return rehomed, logits[0], term[0, 0]


def solution(mesh):
    split = P(ALL)
    return jax.shard_map(
        per_device,
        mesh=mesh,
        in_specs=(split,) * 11 + (P(),) * 10,
        out_specs=(split, split, P()),
        check_vma=False,
    )
```

```python
import functools

import jax
import jax.numpy as jnp
import numpy as np
from jax import lax
from jax.experimental import pallas as pl
from jax.experimental.pallas import tpu as pltpu
from jax.sharding import PartitionSpec as P

ALL = ("hst", "chip")
PERIOD = 13
HOME, ORPHAN = 48, 32
FIXED = 6
SLOTS = 84
ROWS = 88
F = 26
BATCH = 512
NONE = 1023
QW = 896
BF, F32 = jnp.bfloat16, jnp.float32
VMEM = pl.BlockSpec(memory_space=pltpu.VMEM)
SMEM = pl.BlockSpec(memory_space=pltpu.SMEM)


def slot_tables():
    table = np.full((PERIOD, 128), -1, np.int32)
    label = np.full((PERIOD, 3), -1, np.int32)
    for r in range(PERIOD):
        for g in range(PERIOD):
            k = (g - 11 * r) % PERIOD
            o = (g - 4 - 3 * r) % PERIOD
            for e in range(2):
                table[r, FIXED * g + e] = 2 * k + e
                if k + PERIOD < HOME // 2:
                    table[r, FIXED * g + 2 + e] = 2 * (k + PERIOD) + e
                table[r, FIXED * g + 4 + e] = 2 * o + e
        rest = [(PERIOD + i, (4 + 3 * r + i) % PERIOD) for i in range(3)]
        free = [0, 1, 2]
        for k, g in sorted(rest, key=lambda item: item[1] == 0):
            at = g % 3 if g % 3 in free else free[0]
            free.remove(at)
            label[r, at] = g
            for e in range(2):
                table[r, PERIOD * FIXED + 2 * at + e] = 2 * k + e
    for g in range(1, PERIOD):
        assert all(at == g % 3 for r in range(PERIOD) for at in range(3) if label[r, at] == g)
    return table, label


def feature_rows():
    rows = np.full((QW,), 479, np.int32)
    rows[:128] = np.arange(128)
    at = 128
    for a in range(4):
        for tile in range(1 if a < 2 else 2):
            for lane in range(128):
                turn = (lane - 7) % 128
                i, j = 8 * a + turn % 8, 16 * tile + turn // 8
                if j < i <= F:
                    rows[at + lane] = 128 + i * (i - 1) // 2 + j
            at += 128
    return rows


TABLE, LABEL = slot_tables()
FEATURE_ROWS = feature_rows()


def route_kernel(owner, orphans, out, count):
    slots = out.shape[0] // count.shape[0]

    def clear(c, _):
        count[c] = 0
        return 0

    lax.fori_loop(0, count.shape[0], clear, 0)
    out[...] = jnp.zeros_like(out)

    def place(i, _):
        o = owner[i]
        n = count[o]
        out[slots * o + n] = orphans[i]
        count[o] = n + 1
        return 0

    lax.fori_loop(0, orphans.shape[0], place, 0)


def route(orphan_owner, orphans, chips):
    return pl.pallas_call(
        route_kernel,
        out_shape=jax.ShapeDtypeStruct((2 * chips,) + orphans.shape[1:], BF),
        in_specs=[SMEM, VMEM],
        out_specs=VMEM,
        scratch_shapes=[pltpu.SMEM((chips,), jnp.int32)],
        compiler_params=pltpu.CompilerParams(vmem_limit_bytes=16 << 20),
        cost_estimate=pl.CostEstimate(flops=0, transcendentals=0, bytes_accessed=3 << 20),
    )(orphan_owner, orphans)


def pool_kernel(*refs):
    given, out, (wide, sam, ready), held, sem, sent = refs[:8], refs[8], refs[9:12], refs[12:20], refs[20], refs[21]
    cuts = [(n, None) for n in range(2, 8)] + [(0, (0, 12)), (0, (26, 38)), (1, (0, 12))]
    cuts = [cuts, [(0, (12, 26)), (0, (38, 48)), (1, (12, 32))]]
    waves = []
    for wave in cuts:
        copies = []
        for n, cut in wave:
            at = pl.ds(cut[0], cut[1] - cut[0]) if cut else pl.ds(0, given[n].shape[0])
            number = len(copies) + 9 * len(waves)
            copies.append(pltpu.make_async_copy(given[n].at[at], held[n].at[at], sem.at[number]))
            copies[-1].start()
        waves.append(copies)
    home, orphan = (held[0],) + tuple(held[2:5]), (held[1],) + tuple(held[5:8])
    me = lax.axis_index("hst") * lax.axis_size("chip") + lax.axis_index("chip")
    rows = lax.broadcasted_iota(jnp.int32, (128, 128), 0).astype(F32).astype(BF)
    place = lax.broadcasted_iota(jnp.int32, (8, 128), 0)
    one, zero = jnp.ones((), BF), jnp.zeros((), BF)
    sam[...] = jnp.full(sam.shape, NONE, jnp.int32)
    for s in range(SLOTS + 2, ROWS):
        wide[pl.ds(s, 128, stride=ROWS), :] = jnp.zeros((128, 128), F32)
    for copy in waves[0]:
        copy.wait()

    def piece(slot, b, blocks, off, length, samples):
        live = jnp.where(place < length[pl.ds(b, 1), :], off[b], -1).astype(F32).astype(BF)
        counts = jnp.zeros((128, 128), BF)
        for n in range(8):
            counts = counts + jnp.where(rows == live[n : n + 1, :], one, zero)
        sums = lax.dot_general(counts, blocks[b], (((0,), (0,)), ((), ())), preferred_element_type=F32)
        wide[pl.ds(slot, 128, stride=ROWS), :] = sums
        sam[pl.ds(slot, 1), :] = samples[pl.ds(b, 1), :]

    def pair(k, more):
        g = FIXED * lax.rem(11 * me + k, PERIOD)
        for e in range(2):
            piece(g + e, 2 * k + e, *home)
        for e in range(2):
            if more:
                piece(g + 2 + e, 2 * (k + PERIOD) + e, *home)
            else:
                wide[pl.ds(g + 2 + e, 128, stride=ROWS), :] = jnp.zeros((128, 128), F32)
        g = FIXED * lax.rem(4 + 3 * me + k, PERIOD)
        for e in range(2):
            piece(g + 4 + e, 2 * k + e, *orphan)

    def step(k, _):
        pair(k, True)
        return 0

    both = HOME // 2 - PERIOD
    lax.fori_loop(0, 6, step, 0, unroll=6)
    for copy in waves[1]:
        copy.wait()
    lax.fori_loop(6, both, step, 0, unroll=5)
    for k in range(both, PERIOD):
        pair(k, False)
    rest = [lax.rem(4 + 3 * me + i, PERIOD) for i in range(3)]
    for i, g in enumerate(rest):
        others = sum(lax.rem(h, 3) for h in rest if h is not g)
        at = jnp.where(g == 0, 3 - others, lax.rem(g, 3))
        for e in range(2):
            piece(PERIOD * FIXED + 2 * at + e, 2 * (PERIOD + i) + e, *orphan)
    index = sam[...]
    wide[pl.ds(SLOTS, 128, stride=ROWS), :] = (index >> 4).astype(F32).T
    wide[pl.ds(SLOTS + 1, 128, stride=ROWS), :] = (index & 15).astype(F32).T

    parts = sent.shape[0]
    span = 128 // parts
    copies = []
    for n in range(parts):

        def narrow(q, _):
            q = span // 4 * n + q
            ready[pl.ds(4 * q, 4)] = wide[pl.ds(4 * q * ROWS, 4 * ROWS), :].reshape(4, ROWS, 128).astype(BF)
            return 0

        lax.fori_loop(0, span // 4, narrow, 0, unroll=2)
        at = pl.ds(span * n, span)
        copies.append(pltpu.make_async_copy(ready.at[at], out.at[at], sent.at[n]))
        copies[-1].start()
    for copy in copies:
        copy.wait()


def pool(*arrays):
    return pl.pallas_call(
        pool_kernel,
        out_shape=jax.ShapeDtypeStruct((128, ROWS, 128), BF),
        in_specs=[pl.BlockSpec(memory_space=pl.ANY)] * 8,
        out_specs=pl.BlockSpec(memory_space=pl.ANY),
        scratch_shapes=[
            pltpu.VMEM((128 * ROWS, 128), F32),
            pltpu.VMEM((128, 128), jnp.int32),
            pltpu.VMEM((128, ROWS, 128), BF),
        ]
        + [pltpu.VMEM(a.shape, a.dtype) for a in arrays]
        + [pltpu.SemaphoreType.DMA((12,)), pltpu.SemaphoreType.DMA((8,))],
        compiler_params=pltpu.CompilerParams(vmem_limit_bytes=60 << 20),
        cost_estimate=pl.CostEstimate(flops=84 * 128 * 128 * 256, transcendentals=0, bytes_accessed=6 << 20),
    )(*arrays)


def tail_kernel(*refs):
    (given, *others), (logits, loss), refs = refs[:8], refs[8:10], refs[10:]
    recv, (label, bottom, weights, bias, last, last_bias, marks), refs = refs[0], refs[1:8], refs[8:]
    wide, hi, lo, stack, packed, came, sems = refs
    parts = came.shape[0]
    span = 128 // parts
    copies = []
    for n in range(parts):
        at = pl.ds(span * n, span)
        copies.append(pltpu.make_async_copy(given.at[at], recv.at[at], came.at[n]))
        copies[-1].start()
    held = (label, bottom, weights, bias, last, last_bias, marks)
    fetches = [pltpu.make_async_copy(g, h, sems.at[n]) for n, (g, h) in enumerate(zip(others, held))]
    for fetch in fetches:
        fetch.start()
    zero = jnp.zeros((), BF)
    ones = lax.broadcasted_iota(jnp.int32, (16, 128), 0).astype(F32).astype(BF)

    def widen(p, _):
        wide[pl.ds(4 * p * ROWS, 4 * ROWS), :] = recv[pl.ds(4 * p, 4)].astype(F32).reshape(4 * ROWS, 128)
        return 0

    for n in range(parts):
        copies[n].wait()
        lax.fori_loop(span // 4 * n, span // 4 * (n + 1), widen, 0, unroll=2)
    hi[...] = wide[pl.ds(SLOTS, 128, stride=ROWS), :].T
    lo[...] = wide[pl.ds(SLOTS + 1, 128, stride=ROWS), :].T

    for fetch in fetches[:2]:
        fetch.wait()
    stack[0] = bottom[...].astype(BF).astype(F32)

    def hits(slot, keep=None):
        high = hi[pl.ds(slot, 1), :]
        if keep is not None:
            high = jnp.where(keep, high, 63.0)
        high = jnp.broadcast_to(high, (16, 128)).astype(BF)
        low = jnp.broadcast_to(lo[pl.ds(slot, 1), :], (16, 128)).astype(BF)
        low = jnp.where(low == ones, jnp.ones((), BF), zero)
        return jnp.concatenate([jnp.where(high == jnp.asarray(h, BF), low, zero) for h in range(32)], axis=0)

    def rows(slot):
        return wide[pl.ds(slot, 128, stride=ROWS), :].astype(BF)

    def pooled(g, places):
        for e in range(2):
            slots = [(FIXED * g + 2 * n + e, None) for n in range(3)]
            for at in places:
                keep = label[pl.ds(at, 1), :] == jnp.asarray(g, jnp.int32)
                slots.append((PERIOD * FIXED + 2 * at + e, keep))
            left = jnp.concatenate([hits(s, keep) for s, keep in slots], axis=1)
            right = jnp.concatenate([rows(s) for s, _ in slots], axis=0)
            total = jnp.dot(left, right, preferred_element_type=F32)
            stack[1 + 2 * g + e] = total.astype(BF).astype(F32)

    pooled(0, [0, 1, 2])

    def group(g, _):
        pooled(g, [lax.rem(g, 3)])
        return 0

    lax.fori_loop(1, PERIOD, group, 0, unroll=4)

    packed[:, :128] = bottom[...].astype(BF)
    own = lax.broadcasted_iota(jnp.int32, (8, 128), 1) % 8 == 7 - lax.broadcasted_iota(jnp.int32, (8, 128), 0)

    back = 7 - lax.broadcasted_iota(jnp.int32, (8, 128), 0)

    def interact(m, _):
        halves = []
        for half in range(2):
            left = stack[:, pl.ds(16 * m + 8 * half, 8), :].reshape(8 * (F + 1), 128).astype(BF)
            right = [jnp.take_along_axis(stack[j, pl.ds(16 * m + 8 * half, 8), :], back, axis=0) for j in range(F + 1)]
            right = jnp.concatenate(right + [jnp.zeros((8 * (31 - F), 128), F32)], axis=0).astype(BF)
            gram = lax.dot_general(left, right, (((1,), (1,)), ((), ())), preferred_element_type=F32)
            columns = []
            for a in range(4):
                for tile in range(1 if a < 2 else 2):
                    total = None
                    for c in range(8):
                        i = 8 * a + c
                        if i > F or 16 * tile >= i:
                            continue
                        part = jnp.where(own, gram[8 * i : 8 * i + 8, 128 * tile : 128 * tile + 128], 0.0)
                        part = pltpu.roll(part, c, 1, stride=1, stride_axis=0)
                        total = part if total is None else total + part
                    columns.append(total)
            halves.append(jnp.concatenate(columns, axis=1))
        packed[pl.ds(pl.multiple_of(16 * m, 16), 16), 128:] = jnp.concatenate(halves, axis=0).astype(BF)
        return 0

    lax.fori_loop(0, BATCH // 16, interact, 0, unroll=16)

    for fetch in fetches[2:]:
        fetch.wait()
    hidden = jnp.dot(packed[...], weights[...], preferred_element_type=F32)
    hidden = jnp.maximum(hidden + bias[...], 0.0).astype(BF)
    out = lax.dot_general(last[...], hidden, (((1,), (1,)), ((), ())), preferred_element_type=F32)
    x = out[:1] + last_bias[:, :1]
    logits[...] = x
    soft = jnp.maximum(x, 0.0) + jnp.log1p(jnp.exp(-jnp.abs(x)))
    term = jnp.sum(soft - marks[...].astype(F32) * x)
    loss[...] = jnp.full(loss.shape, term, F32)


def tail(given, *others):
    anywhere = pl.BlockSpec(memory_space=pl.ANY)
    return pl.pallas_call(
        tail_kernel,
        out_shape=(jax.ShapeDtypeStruct((1, BATCH), F32), jax.ShapeDtypeStruct((1, 128), F32)),
        in_specs=[anywhere] * 8,
        out_specs=(VMEM, VMEM),
        scratch_shapes=[pltpu.VMEM(a.shape, a.dtype) for a in (given,) + others]
        + [
            pltpu.VMEM((128 * ROWS, 128), F32),
            pltpu.VMEM((128, 128), F32),
            pltpu.VMEM((128, 128), F32),
            pltpu.VMEM((F + 1, BATCH, 128), F32),
            pltpu.VMEM((BATCH, QW), BF),
            pltpu.SemaphoreType.DMA((8,)),
            pltpu.SemaphoreType.DMA((7,)),
        ],
        compiler_params=pltpu.CompilerParams(vmem_limit_bytes=60 << 20),
        cost_estimate=pl.CostEstimate(flops=6 << 30, transcendentals=0, bytes_accessed=5 << 20),
    )(given, *others)


def labels_by_holder():
    label = np.full((8, 128), -1, np.int32)
    label[:3] = LABEL[np.arange(128) % PERIOD].T
    return label


def exchange(value, axes):
    return lax.all_to_all(value, axes, split_axis=0, concat_axis=0, tiled=True)


def ring_sum(value, axis):
    one, two, three = (lax.ppermute(value, axis, [(i, (i + k) % 4) for i in range(4)]) for k in (1, 2, 3))
    return (value + two) + (one + three)


def part_ring(value, axis, size, step):
    one, two, three = (
        lax.ppermute(value, axis, [(i, i - i // step % 4 * step + (i // step + k) % 4 * step) for i in range(size)])
        for k in (1, 2, 3)
    )
    return (value + two) + (one + three)


def keep_kernel(given, out, sent):
    span = given.shape[0] // sent.shape[0]
    copies = []
    for n in range(sent.shape[0]):
        at = pl.ds(span * n, span)
        copies.append(pltpu.make_async_copy(given.at[at], out.at[at], sent.at[n]))
        copies[-1].start()
    for copy in copies:
        copy.wait()


def keep(value):
    return pl.pallas_call(
        keep_kernel,
        out_shape=jax.ShapeDtypeStruct(value.shape, value.dtype),
        in_specs=[VMEM],
        out_specs=pl.BlockSpec(memory_space=pl.ANY),
        scratch_shapes=[pltpu.SemaphoreType.DMA((8,))],
        compiler_params=pltpu.CompilerParams(vmem_limit_bytes=8 << 20),
        cost_estimate=pl.CostEstimate(flops=0, transcendentals=0, bytes_accessed=4 << 20),
    )(value)


def per_device(
    resident_row_blocks,
    orphan_blocks,
    home_offsets,
    home_lengths,
    home_samples,
    orphan_offsets,
    orphan_lengths,
    orphan_samples,
    orphan_owner,
    dense_inputs,
    labels,
    bottom_first,
    bias_first,
    bottom_second,
    bias_second,
    bottom_third,
    bias_third,
    top_hidden,
    bias_hidden,
    top_logit,
    bias_logit,
):
    chips = lax.axis_size("chip")
    outgoing = route(orphan_owner[:, 0], orphan_blocks, chips)
    pieces = pool(
        resident_row_blocks,
        orphan_blocks,
        home_offsets.transpose(0, 2, 1),
        home_lengths,
        home_samples,
        orphan_offsets.transpose(0, 2, 1),
        orphan_lengths,
        orphan_samples,
    )
    arrived = exchange(pieces, ALL)
    first = jax.nn.relu(
        jnp.dot(dense_inputs, bottom_first, preferred_element_type=F32) + bias_first
    ).astype(BF)
    second = jax.nn.relu(
        jnp.dot(first, bottom_second, preferred_element_type=F32) + bias_second
    ).astype(BF)
    bottom = jax.nn.relu(jnp.dot(second, bottom_third, preferred_element_type=F32) + bias_third)
    padded = jnp.concatenate([top_hidden, jnp.zeros((1, top_hidden.shape[1]), BF)], axis=0)
    weights = jnp.take(padded, jnp.asarray(FEATURE_ROWS), axis=0)
    last = jnp.broadcast_to(top_logit.reshape(1, -1), (8, top_logit.shape[0]))
    last_bias = jnp.broadcast_to(bias_logit[None, :], (1, 128))
    outgoing, weights, bottom, last, last_bias = lax.optimization_barrier(
        (outgoing, weights, bottom, last, last_bias)
    )
    rehomed = exchange(outgoing, "chip")
    logits, term = tail(
        arrived,
        jnp.asarray(labels_by_holder()),
        bottom,
        weights,
        bias_hidden[None, :],
        last,
        last_bias,
        labels[None, :],
    )
    term = ring_sum(term, "hst")
    term = term + lax.ppermute(term, "chip", [(i, i ^ 1) for i in range(chips)])
    term = part_ring(term, "chip", chips, 2)
    rehomed, term = lax.optimization_barrier((keep(rehomed), term))
    term = part_ring(term, "chip", chips, 8)
    return rehomed, logits[0], term[0, 0]


def solution(mesh):
    split = P(ALL)
    return jax.shard_map(
        per_device,
        mesh=mesh,
        in_specs=(split,) * 11 + (P(),) * 10,
        out_specs=(split, split, P()),
        check_vma=False,
    )
```

```python
import functools

import jax
import jax.numpy as jnp
import numpy as np
from jax import lax
from jax.experimental import pallas as pl
from jax.experimental.pallas import tpu as pltpu
from jax.sharding import PartitionSpec as P

ALL = ("hst", "chip")
PERIOD = 13
HOME, ORPHAN = 48, 32
FIXED = 6
SLOTS = 84
ROWS = 88
F = 26
BATCH = 512
NONE = 1023
QW = 896
BF, F32 = jnp.bfloat16, jnp.float32
VMEM = pl.BlockSpec(memory_space=pltpu.VMEM)
SMEM = pl.BlockSpec(memory_space=pltpu.SMEM)


def slot_tables():
    table = np.full((PERIOD, 128), -1, np.int32)
    label = np.full((PERIOD, 3), -1, np.int32)
    for r in range(PERIOD):
        for g in range(PERIOD):
            k = (g - 11 * r) % PERIOD
            o = (g - 4 - 3 * r) % PERIOD
            for e in range(2):
                table[r, FIXED * g + e] = 2 * k + e
                if k + PERIOD < HOME // 2:
                    table[r, FIXED * g + 2 + e] = 2 * (k + PERIOD) + e
                table[r, FIXED * g + 4 + e] = 2 * o + e
        rest = [(PERIOD + i, (4 + 3 * r + i) % PERIOD) for i in range(3)]
        free = [0, 1, 2]
        for k, g in sorted(rest, key=lambda item: item[1] == 0):
            at = g % 3 if g % 3 in free else free[0]
            free.remove(at)
            label[r, at] = g
            for e in range(2):
                table[r, PERIOD * FIXED + 2 * at + e] = 2 * k + e
    for g in range(1, PERIOD):
        assert all(at == g % 3 for r in range(PERIOD) for at in range(3) if label[r, at] == g)
    return table, label


def feature_rows():
    rows = np.full((QW,), 479, np.int32)
    rows[:128] = np.arange(128)
    at = 128
    for a in range(4):
        for tile in range(1 if a < 2 else 2):
            for lane in range(128):
                turn = (lane - 7) % 128
                i, j = 8 * a + turn % 8, 16 * tile + turn // 8
                if j < i <= F:
                    rows[at + lane] = 128 + i * (i - 1) // 2 + j
            at += 128
    return rows


TABLE, LABEL = slot_tables()
FEATURE_ROWS = feature_rows()


def route_kernel(owner, orphans, out, count):
    slots = out.shape[0] // count.shape[0]

    def clear(c, _):
        count[c] = 0
        return 0

    lax.fori_loop(0, count.shape[0], clear, 0)
    out[...] = jnp.zeros_like(out)

    def place(i, _):
        o = owner[i]
        n = count[o]
        out[slots * o + n] = orphans[i]
        count[o] = n + 1
        return 0

    lax.fori_loop(0, orphans.shape[0], place, 0)


def route(orphan_owner, orphans, chips):
    return pl.pallas_call(
        route_kernel,
        out_shape=jax.ShapeDtypeStruct((2 * chips,) + orphans.shape[1:], BF),
        in_specs=[SMEM, VMEM],
        out_specs=VMEM,
        scratch_shapes=[pltpu.SMEM((chips,), jnp.int32)],
        compiler_params=pltpu.CompilerParams(vmem_limit_bytes=16 << 20),
        cost_estimate=pl.CostEstimate(flops=0, transcendentals=0, bytes_accessed=3 << 20),
    )(orphan_owner, orphans)


def pool_kernel(*refs):
    given, out, (wide, sam, ready), held, sem, sent = refs[:8], refs[8], refs[9:12], refs[12:20], refs[20], refs[21]
    cuts = [(n, None) for n in range(2, 8)] + [(0, (0, 12)), (0, (26, 38)), (1, (0, 12))]
    cuts = [cuts, [(0, (12, 26)), (0, (38, 48)), (1, (12, 32))]]
    waves = []
    for wave in cuts:
        copies = []
        for n, cut in wave:
            at = pl.ds(cut[0], cut[1] - cut[0]) if cut else pl.ds(0, given[n].shape[0])
            number = len(copies) + 9 * len(waves)
            copies.append(pltpu.make_async_copy(given[n].at[at], held[n].at[at], sem.at[number]))
            copies[-1].start()
        waves.append(copies)
    home, orphan = (held[0],) + tuple(held[2:5]), (held[1],) + tuple(held[5:8])
    me = lax.axis_index("hst") * lax.axis_size("chip") + lax.axis_index("chip")
    rows = lax.broadcasted_iota(jnp.int32, (128, 128), 0).astype(F32).astype(BF)
    place = lax.broadcasted_iota(jnp.int32, (8, 128), 0)
    one, zero = jnp.ones((), BF), jnp.zeros((), BF)
    sam[...] = jnp.full(sam.shape, NONE, jnp.int32)
    for s in range(SLOTS + 2, ROWS):
        wide[pl.ds(s, 128, stride=ROWS), :] = jnp.zeros((128, 128), F32)
    for copy in waves[0]:
        copy.wait()

    def piece(slot, b, blocks, off, length, samples):
        live = jnp.where(place < length[pl.ds(b, 1), :], off[b], -1).astype(F32).astype(BF)
        counts = jnp.zeros((128, 128), BF)
        for n in range(8):
            counts = counts + jnp.where(rows == live[n : n + 1, :], one, zero)
        sums = lax.dot_general(counts, blocks[b], (((0,), (0,)), ((), ())), preferred_element_type=F32)
        wide[pl.ds(slot, 128, stride=ROWS), :] = sums
        sam[pl.ds(slot, 1), :] = samples[pl.ds(b, 1), :]

    def pair(k, more):
        g = FIXED * lax.rem(11 * me + k, PERIOD)
        for e in range(2):
            piece(g + e, 2 * k + e, *home)
        for e in range(2):
            if more:
                piece(g + 2 + e, 2 * (k + PERIOD) + e, *home)
            else:
                wide[pl.ds(g + 2 + e, 128, stride=ROWS), :] = jnp.zeros((128, 128), F32)
        g = FIXED * lax.rem(4 + 3 * me + k, PERIOD)
        for e in range(2):
            piece(g + 4 + e, 2 * k + e, *orphan)

    def step(k, _):
        pair(k, True)
        return 0

    both = HOME // 2 - PERIOD
    lax.fori_loop(0, 6, step, 0, unroll=6)
    for copy in waves[1]:
        copy.wait()
    lax.fori_loop(6, both, step, 0, unroll=5)
    for k in range(both, PERIOD):
        pair(k, False)
    rest = [lax.rem(4 + 3 * me + i, PERIOD) for i in range(3)]
    for i, g in enumerate(rest):
        others = sum(lax.rem(h, 3) for h in rest if h is not g)
        at = jnp.where(g == 0, 3 - others, lax.rem(g, 3))
        for e in range(2):
            piece(PERIOD * FIXED + 2 * at + e, 2 * (PERIOD + i) + e, *orphan)
    index = sam[...]
    wide[pl.ds(SLOTS, 128, stride=ROWS), :] = (index >> 4).astype(F32).T
    wide[pl.ds(SLOTS + 1, 128, stride=ROWS), :] = (index & 15).astype(F32).T

    parts = sent.shape[0]
    span = 128 // parts
    copies = []
    for n in range(parts):

        def narrow(q, _):
            q = span // 4 * n + q
            ready[pl.ds(4 * q, 4)] = wide[pl.ds(4 * q * ROWS, 4 * ROWS), :].reshape(4, ROWS, 128).astype(BF)
            return 0

        lax.fori_loop(0, span // 4, narrow, 0, unroll=2)
        at = pl.ds(span * n, span)
        copies.append(pltpu.make_async_copy(ready.at[at], out.at[at], sent.at[n]))
        copies[-1].start()
    for copy in copies:
        copy.wait()


def pool(*arrays):
    return pl.pallas_call(
        pool_kernel,
        out_shape=jax.ShapeDtypeStruct((128, ROWS, 128), BF),
        in_specs=[pl.BlockSpec(memory_space=pl.ANY)] * 8,
        out_specs=pl.BlockSpec(memory_space=pl.ANY),
        scratch_shapes=[
            pltpu.VMEM((129 * ROWS, 128), F32),
            pltpu.VMEM((128, 128), jnp.int32),
            pltpu.VMEM((128, ROWS, 128), BF),
        ]
        + [pltpu.VMEM(a.shape, a.dtype) for a in arrays]
        + [pltpu.SemaphoreType.DMA((12,)), pltpu.SemaphoreType.DMA((8,))],
        compiler_params=pltpu.CompilerParams(vmem_limit_bytes=60 << 20),
        cost_estimate=pl.CostEstimate(flops=84 * 128 * 128 * 256, transcendentals=0, bytes_accessed=6 << 20),
    )(*arrays)


def tail_kernel(*refs):
    (given, *others), (logits, loss), refs = refs[:8], refs[8:10], refs[10:]
    recv, (label, bottom, weights, bias, last, last_bias, marks), refs = refs[0], refs[1:8], refs[8:]
    wide, hi, lo, stack, packed, came, sems = refs
    parts = came.shape[0]
    span = 128 // parts
    copies = []
    for n in range(parts):
        at = pl.ds(span * n, span)
        copies.append(pltpu.make_async_copy(given.at[at], recv.at[at], came.at[n]))
        copies[-1].start()
    held = (label, bottom, weights, bias, last, last_bias, marks)
    fetches = [pltpu.make_async_copy(g, h, sems.at[n]) for n, (g, h) in enumerate(zip(others, held))]
    for fetch in fetches:
        fetch.start()
    zero = jnp.zeros((), BF)
    ones = lax.broadcasted_iota(jnp.int32, (16, 128), 0).astype(F32).astype(BF)

    def widen(p, _):
        wide[pl.ds(4 * p * ROWS, 4 * ROWS), :] = recv[pl.ds(4 * p, 4)].astype(F32).reshape(4 * ROWS, 128)
        return 0

    for n in range(parts):
        copies[n].wait()
        lax.fori_loop(span // 4 * n, span // 4 * (n + 1), widen, 0, unroll=2)
    hi[...] = wide[pl.ds(SLOTS, 128, stride=ROWS), :].T
    lo[...] = wide[pl.ds(SLOTS + 1, 128, stride=ROWS), :].T

    for fetch in fetches[:2]:
        fetch.wait()
    stack[0] = bottom[...].astype(BF).astype(F32)

    def hits(slot, keep=None):
        high = hi[pl.ds(slot, 1), :]
        if keep is not None:
            high = jnp.where(keep, high, 63.0)
        high = jnp.broadcast_to(high, (16, 128)).astype(BF)
        low = jnp.broadcast_to(lo[pl.ds(slot, 1), :], (16, 128)).astype(BF)
        low = jnp.where(low == ones, jnp.ones((), BF), zero)
        return jnp.concatenate([jnp.where(high == jnp.asarray(h, BF), low, zero) for h in range(32)], axis=0)

    def rows(slot):
        return wide[pl.ds(slot, 128, stride=ROWS), :].astype(BF)

    def pooled(g, places):
        for e in range(2):
            slots = [(FIXED * g + 2 * n + e, None) for n in range(3)]
            for at in places:
                keep = label[pl.ds(at, 1), :] == jnp.asarray(g, jnp.int32)
                slots.append((PERIOD * FIXED + 2 * at + e, keep))
            left = jnp.concatenate([hits(s, keep) for s, keep in slots], axis=1)
            right = jnp.concatenate([rows(s) for s, _ in slots], axis=0)
            total = jnp.dot(left, right, preferred_element_type=F32)
            stack[1 + 2 * g + e] = total.astype(BF).astype(F32)

    pooled(0, [0, 1, 2])

    def group(g, _):
        pooled(g, [lax.rem(g, 3)])
        return 0

    lax.fori_loop(1, PERIOD, group, 0, unroll=4)

    packed[:, :128] = bottom[...].astype(BF)
    own = lax.broadcasted_iota(jnp.int32, (8, 128), 1) % 8 == 7 - lax.broadcasted_iota(jnp.int32, (8, 128), 0)

    back = 7 - lax.broadcasted_iota(jnp.int32, (8, 128), 0)

    def interact(m, _):
        halves = []
        for half in range(2):
            left = stack[:, pl.ds(16 * m + 8 * half, 8), :].reshape(8 * (F + 1), 128).astype(BF)
            right = [jnp.take_along_axis(stack[j, pl.ds(16 * m + 8 * half, 8), :], back, axis=0) for j in range(F + 1)]
            right = jnp.concatenate(right + [jnp.zeros((8 * (31 - F), 128), F32)], axis=0).astype(BF)
            gram = lax.dot_general(left, right, (((1,), (1,)), ((), ())), preferred_element_type=F32)
            columns = []
            for a in range(4):
                for tile in range(1 if a < 2 else 2):
                    total = None
                    for c in range(8):
                        i = 8 * a + c
                        if i > F or 16 * tile >= i:
                            continue
                        part = jnp.where(own, gram[8 * i : 8 * i + 8, 128 * tile : 128 * tile + 128], 0.0)
                        part = pltpu.roll(part, c, 1, stride=1, stride_axis=0)
                        total = part if total is None else total + part
                    columns.append(total)
            halves.append(jnp.concatenate(columns, axis=1))
        packed[pl.ds(pl.multiple_of(16 * m, 16), 16), 128:] = jnp.concatenate(halves, axis=0).astype(BF)
        return 0

    lax.fori_loop(0, BATCH // 16, interact, 0, unroll=16)

    for fetch in fetches[2:]:
        fetch.wait()
    hidden = jnp.dot(packed[...], weights[...], preferred_element_type=F32)
    hidden = jnp.maximum(hidden + bias[...], 0.0).astype(BF)
    out = lax.dot_general(last[...], hidden, (((1,), (1,)), ((), ())), preferred_element_type=F32)
    x = out[:1] + last_bias[:, :1]
    logits[...] = x
    soft = jnp.maximum(x, 0.0) + jnp.log1p(jnp.exp(-jnp.abs(x)))
    term = jnp.sum(soft - marks[...].astype(F32) * x)
    loss[...] = jnp.full(loss.shape, term, F32)


def tail(given, *others):
    anywhere = pl.BlockSpec(memory_space=pl.ANY)
    return pl.pallas_call(
        tail_kernel,
        out_shape=(jax.ShapeDtypeStruct((1, BATCH), F32), jax.ShapeDtypeStruct((1, 128), F32)),
        in_specs=[anywhere] * 8,
        out_specs=(VMEM, VMEM),
        scratch_shapes=[pltpu.VMEM(a.shape, a.dtype) for a in (given,) + others]
        + [
            pltpu.VMEM((129 * ROWS, 128), F32),
            pltpu.VMEM((128, 128), F32),
            pltpu.VMEM((128, 128), F32),
            pltpu.VMEM((F + 1, BATCH, 128), F32),
            pltpu.VMEM((BATCH, QW), BF),
            pltpu.SemaphoreType.DMA((8,)),
            pltpu.SemaphoreType.DMA((7,)),
        ],
        compiler_params=pltpu.CompilerParams(vmem_limit_bytes=60 << 20),
        cost_estimate=pl.CostEstimate(flops=6 << 30, transcendentals=0, bytes_accessed=5 << 20),
    )(given, *others)


def labels_by_holder():
    label = np.full((8, 128), -1, np.int32)
    label[:3] = LABEL[np.arange(128) % PERIOD].T
    return label


def exchange(value, axes):
    return lax.all_to_all(value, axes, split_axis=0, concat_axis=0, tiled=True)


def ring_sum(value, axis):
    one, two, three = (lax.ppermute(value, axis, [(i, (i + k) % 4) for i in range(4)]) for k in (1, 2, 3))
    return (value + two) + (one + three)


def part_ring(value, axis, size, step):
    one, two, three = (
        lax.ppermute(value, axis, [(i, i - i // step % 4 * step + (i // step + k) % 4 * step) for i in range(size)])
        for k in (1, 2, 3)
    )
    return (value + two) + (one + three)


def keep_kernel(given, out, sent):
    span = given.shape[0] // sent.shape[0]
    copies = []
    for n in range(sent.shape[0]):
        at = pl.ds(span * n, span)
        copies.append(pltpu.make_async_copy(given.at[at], out.at[at], sent.at[n]))
        copies[-1].start()
    for copy in copies:
        copy.wait()


def keep(value):
    return pl.pallas_call(
        keep_kernel,
        out_shape=jax.ShapeDtypeStruct(value.shape, value.dtype),
        in_specs=[VMEM],
        out_specs=pl.BlockSpec(memory_space=pl.ANY),
        scratch_shapes=[pltpu.SemaphoreType.DMA((8,))],
        compiler_params=pltpu.CompilerParams(vmem_limit_bytes=8 << 20),
        cost_estimate=pl.CostEstimate(flops=0, transcendentals=0, bytes_accessed=4 << 20),
    )(value)


def per_device(
    resident_row_blocks,
    orphan_blocks,
    home_offsets,
    home_lengths,
    home_samples,
    orphan_offsets,
    orphan_lengths,
    orphan_samples,
    orphan_owner,
    dense_inputs,
    labels,
    bottom_first,
    bias_first,
    bottom_second,
    bias_second,
    bottom_third,
    bias_third,
    top_hidden,
    bias_hidden,
    top_logit,
    bias_logit,
):
    chips = lax.axis_size("chip")
    outgoing = route(orphan_owner[:, 0], orphan_blocks, chips)
    pieces = pool(
        resident_row_blocks,
        orphan_blocks,
        home_offsets.transpose(0, 2, 1),
        home_lengths,
        home_samples,
        orphan_offsets.transpose(0, 2, 1),
        orphan_lengths,
        orphan_samples,
    )
    arrived = exchange(pieces, ALL)
    first = jax.nn.relu(
        jnp.dot(dense_inputs, bottom_first, preferred_element_type=F32) + bias_first
    ).astype(BF)
    second = jax.nn.relu(
        jnp.dot(first, bottom_second, preferred_element_type=F32) + bias_second
    ).astype(BF)
    bottom = jax.nn.relu(jnp.dot(second, bottom_third, preferred_element_type=F32) + bias_third)
    padded = jnp.concatenate([top_hidden, jnp.zeros((1, top_hidden.shape[1]), BF)], axis=0)
    weights = jnp.take(padded, jnp.asarray(FEATURE_ROWS), axis=0)
    last = jnp.broadcast_to(top_logit.reshape(1, -1), (8, top_logit.shape[0]))
    last_bias = jnp.broadcast_to(bias_logit[None, :], (1, 128))
    outgoing, weights, bottom, last, last_bias = lax.optimization_barrier(
        (outgoing, weights, bottom, last, last_bias)
    )
    rehomed = exchange(outgoing, "chip")
    logits, term = tail(
        arrived,
        jnp.asarray(labels_by_holder()),
        bottom,
        weights,
        bias_hidden[None, :],
        last,
        last_bias,
        labels[None, :],
    )
    term = ring_sum(term, "hst")
    term = term + lax.ppermute(term, "chip", [(i, i ^ 1) for i in range(chips)])
    term = part_ring(term, "chip", chips, 2)
    rehomed, term = lax.optimization_barrier((keep(rehomed), term))
    term = part_ring(term, "chip", chips, 8)
    return rehomed, logits[0], term[0, 0]


def solution(mesh):
    split = P(ALL)
    return jax.shard_map(
        per_device,
        mesh=mesh,
        in_specs=(split,) * 11 + (P(),) * 10,
        out_specs=(split, split, P()),
        check_vma=False,
    )
```
